32 devices in a mesh: gx: 4 (over z), gy: 8 (over y, x, core).
Axes of the slice: x: 2, y: 2, z: 4, core: 2. Of those that a mesh axis runs over, the one named last changes fastest.
Arguments:
- orbitals: bfloat16 [24, 48, 11, 256], P('gx', 'gy'), may hold values from -140 to 140, as said below
- masses: float32 [24, 48, 11], P('gx', 'gy'), may hold values from 0.5 to 2, as said below
- cell_matrices: bfloat16 [4, 8, 2, 216, 216], P('gx', 'gy'), may hold values from -0.12 to 3.12, as said below
Outputs:
- filtered_orbitals: bfloat16 [24, 48, 11, 256], P('gx', 'gy')
The draws below stay inside these ranges and needn't reach their ends.
Inputs may be any that keep to these rules, and one draw needn't show every extreme that they name: Entries of orbitals that hold the same mesh node are equal. Entries of masses that hold the same mesh node are equal. `cell_matrices`: every cell matrix is symmetric.
All inputs are finite; a program needn't handle non-finite values.
Results may differ from the reference program's by a relative error of at most 0.0063.
The reference program's roundings to bfloat16 on the way count: a program that leaves them out, or rounds other values in their place, can miss the bound.
Values sent between devices are 32-bit elements; how exact they have to be, the bound alone decides.
A program may use at most 64 MiB of HBM per device.

```python
import math
import jax
import jax.numpy as jnp
from jax import lax

ORBS = 256
CX = 1
CY = 1
CZ = 2
FILTER_DEG = 3
NS_STEPS = 2
N_GX = 4
N_GY = 8


def repeat_rims_drawn(array, along_dim, device_count, cells_along):
    layers = 5 * cells_along
    positions = jnp.arange(device_count * (layers + 1), dtype=jnp.int32)
    source = (positions // (layers + 1) * layers + positions % (layers + 1)) % (device_count * layers)
    return jnp.take(array, source.astype(jnp.int32), axis=along_dim)


def draw_orbitals(key, part):
    nodes_x = 5 * CX * N_GX
    nodes_y = 5 * CY * N_GY
    depth = 5 * CZ + 1
    shape = (nodes_x, nodes_y, depth, ORBS)
    value_key = jax.random.fold_in(key, 11)
    pair_key = jax.random.fold_in(key, 12)
    values = jnp.clip(jax.random.normal(value_key, shape, jnp.float32), -4.0, 4.0)
    pairing = jax.random.permutation(pair_key, N_GY)
    column_block = jnp.arange(nodes_y, dtype=jnp.int32) // (5 * CY)
    orbital_group = jnp.arange(ORBS, dtype=jnp.int32) % N_GY
    spiked = pairing[column_block][:, None] == orbital_group[None, :]
    values = values * jnp.where(spiked, 8.0, 1.0)[None, :, None, :]
    values = repeat_rims_drawn(values, 0, N_GX, CX)
    values = repeat_rims_drawn(values, 1, N_GY, CY)
    return values.astype(jnp.bfloat16)


def draw_masses(key, part):
    nodes_x = 5 * CX * N_GX
    nodes_y = 5 * CY * N_GY
    depth = 5 * CZ + 1
    shape = (nodes_x, nodes_y, depth)
    mass_key = jax.random.fold_in(key, 21)
    values = jnp.exp(jax.random.uniform(mass_key, shape, jnp.float32, math.log(0.5), math.log(2.0)))
    values = repeat_rims_drawn(values, 0, N_GX, CX)
    values = repeat_rims_drawn(values, 1, N_GY, CY)
    return values.astype(jnp.float32)


def draw_cell_matrices(key, part):
    shape = (CX * N_GX, CY * N_GY, CZ, 216, 216)
    noise_key = jax.random.fold_in(key, 31)
    diag_key = jax.random.fold_in(key, 32)
    noise = 0.03 * jnp.clip(jax.random.normal(noise_key, shape, jnp.float32), -4.0, 4.0)
    symmetric = 0.5 * (noise + jnp.swapaxes(noise, -1, -2))
    diagonal = jax.random.uniform(diag_key, shape[:-1], jnp.float32, 1.5, 3.0)
    identity = jnp.eye(216, dtype=jnp.float32)
    return (symmetric + identity * diagonal[..., None]).astype(jnp.bfloat16)


def setup_inputs(seed: int = 0) -> dict:
    arg_keys = jax.random.split(jax.random.key(seed), 4)
    return {
        "orbitals": draw_orbitals(jax.random.fold_in(arg_keys[3], 71), 0),
        "masses": draw_masses(jax.random.fold_in(arg_keys[3], 71), 0),
        "cell_matrices": draw_cell_matrices(jax.random.fold_in(arg_keys[3], 71), 0),
    }


center_shift = 12.0
half_span = 12.0

def unfold_cells(values, along_dim, cells_along):
    moved = jnp.moveaxis(values, along_dim, 0)
    trailing = moved.shape[1:]
    main_part = moved[:5 * cells_along].reshape((cells_along, 5) + trailing)
    far_layer = moved[5::5][:, None]
    window = jnp.concatenate([main_part, far_layer], 1)
    return jnp.moveaxis(window, (0, 1), (along_dim, along_dim + 1))

def fold_cells(window, along_dim, cells_along):
    moved = jnp.moveaxis(window, (along_dim, along_dim + 1), (0, 1))
    trailing = moved.shape[2:]
    leading = jnp.concatenate([moved[:, :5], jnp.zeros((1, 5) + trailing, moved.dtype)], 0)
    carried = jnp.concatenate([jnp.zeros((1,) + trailing, moved.dtype), moved[:, 5]], 0)
    leading = leading.at[:, 0].add(carried)
    flattened = leading.reshape((5 * (cells_along + 1),) + trailing)[:5 * cells_along + 1]
    return jnp.moveaxis(flattened, 0, along_dim)

def to_cells(values, cells_x, cells_y, cells_z):
    window = unfold_cells(values, 0, cells_x)
    window = unfold_cells(window, 2, cells_y)
    window = unfold_cells(window, 4, cells_z)
    window = jnp.transpose(window, (0, 2, 4, 1, 3, 5, 6))
    return window.reshape((cells_x, cells_y, cells_z, 216, window.shape[-1]))

def from_cells(products, cells_x, cells_y, cells_z):
    window = products.reshape((cells_x, cells_y, cells_z, 6, 6, 6, products.shape[-1]))
    window = jnp.transpose(window, (0, 3, 1, 4, 2, 5, 6))
    window = fold_cells(window, 4, cells_z)
    window = fold_cells(window, 2, cells_y)
    return fold_cells(window, 0, cells_x)

def inverse_root(intersection):
    frob_norm = jnp.sqrt(jnp.sum(intersection * intersection))
    current = intersection / frob_norm
    identity = jnp.eye(intersection.shape[0], dtype=jnp.float32)
    factor_z = identity
    for sweep_index in range(NS_STEPS):
        step_t = 1.5 * identity - 0.5 * jnp.dot(factor_z, current, precision=lax.Precision.HIGHEST)
        current = jnp.dot(current, step_t, precision=lax.Precision.HIGHEST)
        factor_z = jnp.dot(step_t, factor_z, precision=lax.Precision.HIGHEST)
    return factor_z / jnp.sqrt(frob_norm)

def interior(array, layers_x, layers_y):
    trailing = array.shape[2:]
    first_count = array.shape[0] // layers_x
    second_count = array.shape[1] // layers_y
    blocked = array.reshape((first_count, layers_x, second_count, layers_y) + trailing)
    blocked = blocked[:, :layers_x - 1, :, :layers_y - 1]
    return blocked.reshape((first_count * (layers_x - 1), second_count * (layers_y - 1)) + trailing)

def repeat_rims(array, along_dim, device_count, cells_along):
    layers = 5 * cells_along
    positions = jnp.arange(device_count * (layers + 1), dtype=jnp.int32)
    source = (positions // (layers + 1) * layers + positions % (layers + 1)) % (device_count * layers)
    return jnp.take(array, source.astype(jnp.int32), axis=along_dim)

def reference(orbitals, masses, cell_matrices):
    cells_gx, cells_gy, cells_z = cell_matrices.shape[:3]
    layers_x = 5 * CX + 1
    layers_y = 5 * CY + 1
    nodes_x = 5 * cells_gx
    nodes_y = 5 * cells_gy
    depth = orbitals.shape[2]
    orb_count = orbitals.shape[3]
    node_field = interior(orbitals, layers_x, layers_y)
    node_mass = interior(masses, layers_x, layers_y)
    matrices = cell_matrices.astype(jnp.float32)

    def apply_operator(values):
        extended = jnp.concatenate([values, values[:1]], 0)
        extended = jnp.concatenate([extended, extended[:, :1]], 1)
        cell_vectors = to_cells(extended, cells_gx, cells_gy, cells_z)
        products = jnp.einsum('abcij,abcjo->abcio', matrices, cell_vectors, precision=lax.Precision.HIGHEST)
        assembled = from_cells(products, cells_gx, cells_gy, cells_z)
        assembled = assembled[:nodes_x].at[0].add(assembled[nodes_x])
        assembled = assembled[:, :nodes_y].at[:, 0].add(assembled[:, nodes_y])
        return assembled / node_mass[..., None]
    block_width = math.gcd(orb_count, 32)
    orbital_blocks = jnp.moveaxis(node_field.reshape((nodes_x, nodes_y, depth, orb_count // block_width, block_width)), 3, 0)

    def filter_block(block):
        starting = block.astype(jnp.float32)
        previous = starting
        current = (apply_operator(starting) - center_shift * starting) / half_span
        for sweep_index in range(FILTER_DEG - 1):
            rounded = lax.optimization_barrier(current.astype(jnp.bfloat16)).astype(jnp.float32)
            following = 2.0 * (apply_operator(rounded) - center_shift * current) / half_span - previous
            previous = current
            current = following
        return current
    filtered = lax.map(filter_block, orbital_blocks)
    filtered = jnp.moveaxis(filtered, 0, 3).reshape((nodes_x, nodes_y, depth, orb_count))
    node_rows = filtered.reshape((-1, orb_count))
    weighted = node_rows * node_mass.reshape((-1, 1))
    intersection = jnp.einsum('no,np->op', weighted, node_rows, precision=lax.Precision.HIGHEST) / (nodes_x * nodes_y * depth)
    factor = inverse_root(intersection)
    result = jnp.dot(node_rows, factor, precision=lax.Precision.HIGHEST).astype(jnp.bfloat16)
    result = result.reshape((nodes_x, nodes_y, depth, orb_count))
    result = repeat_rims(result, 0, N_GX, CX)
    result = repeat_rims(result, 1, N_GY, CY)
    return result
```

```python
import functools

import jax
import jax.numpy as jnp
import numpy as np
from jax import lax
from jax.experimental import pallas as pl
from jax.experimental.pallas import tpu as pltpu
from jax.sharding import PartitionSpec as P

FILTER_DEG = 3
CENTER_SHIFT = 12.0
HALF_SPAN = 12.0

RIM = 240
ROWS = 432
INNER = ROWS - RIM
CORNERS = 48
PIECES = 1
VMEM_BYTES = 24 << 20
BF16 = jnp.bfloat16
F32 = jnp.float32

MESSAGES = (
    (-1, -1, "corner", 0, 3),
    (1, -1, "corner", 1, 2),
    (-1, 1, "corner", 2, 1),
    (1, 1, "corner", 3, 0),
    (-1, 0, "x", 0, 1),
    (1, 0, "x", 1, 0),
    (0, -1, "y", 0, 1),
    (0, 1, "y", 1, 0),
)


def column_starts():
    starts = {(0, 0): 0, (5, 0): 12, (0, 5): 24, (5, 5): 36}
    for i in range(4):
        starts[(0, i + 1)] = 48 + 12 * i
        starts[(5, i + 1)] = 96 + 12 * i
        starts[(i + 1, 0)] = 144 + 12 * i
        starts[(i + 1, 5)] = 192 + 12 * i
    for i in range(4):
        for j in range(4):
            starts[(i + 1, j + 1)] = RIM + 12 * (4 * i + j)
    return starts


STARTS = column_starts()


def tables():
    down = np.zeros((ROWS, 128), np.int32)
    along = np.full((8, ROWS), -1, np.int32)
    for (x, y), start in STARTS.items():
        for half in range(2):
            for k in range(6):
                row, z = start + 6 * half + k, 5 * half + k
                for cell in range(2):
                    inside = 0 <= z - 5 * cell <= 5
                    down[row, cell] = (x * 6 + y) * 6 + z - 5 * cell if inside else -1
                down[row, 2], down[row, 3] = 8 * x + y, z
                down[row, 4] = int(x < 5 and y < 5 and not (half == 1 and k == 0))
                along[half, row] = (x * 6 + y) * 6 + k
    return down, along


def dot(a, b):
    return jnp.dot(a, b, preferred_element_type=F32)


def dot_rows(a, b):
    return lax.dot_general(a, b, (((0,), (0,)), ((), ())), preferred_element_type=F32)


def split(a):
    high = a.astype(BF16)
    return high, (a - high.astype(F32)).astype(BF16)


def dot3(a, b):
    a_high, a_low = split(a)
    b_high, b_low = split(b)
    return dot(a_high, b_high) + (dot(a_high, b_low) + dot(a_low, b_high))


def one_hot(condition):
    return jnp.where(condition, 1.0, 0.0).astype(F32)


def gram(rows, weight):
    a_high, a_low = split(rows * weight)
    b_high, b_low = split(rows)

    def part(lanes, columns):
        return dot_rows(a_high[:, lanes], b_high[:, columns]) + (
            dot_rows(a_high[:, lanes], b_low[:, columns])
            + dot_rows(a_low[:, lanes], b_high[:, columns])
        )

    top = part(slice(0, 128), slice(0, 256))
    return top[:, :128], top[:, 128:], part(slice(128, 256), slice(128, 256))


def block_ids():
    return (
        lax.broadcasted_iota(jnp.int32, (128, 128), 0),
        lax.broadcasted_iota(jnp.int32, (128, 128), 1),
    )


def pack(grams):
    s00, s01, s11 = grams
    row, col = block_ids()
    diagonal = jnp.sum(jnp.where(row == col, s11, 0.0), axis=0, keepdims=True)
    return jnp.concatenate([s01, jnp.where(row <= col, s00, s11)], axis=0), diagonal


def unpack(packed, diagonal):
    s01, both = packed[0:128], packed[128:256]
    row, col = block_ids()
    upper = jnp.where(row <= col, both, 0.0)
    lower = jnp.where(row > col, both, 0.0)
    s00 = upper + jnp.where(row < col, both, 0.0).T
    s11 = lower + lower.T + jnp.where(row == col, diagonal, 0.0)
    return jnp.concatenate([s00, s01, s11], axis=0)


def inverse_root(stacked, node_total):
    s00, s01, s11 = stacked[0:128], stacked[128:256], stacked[256:384]
    top = jnp.concatenate([s00, s01], axis=1)
    bottom = jnp.concatenate([s01.T, s11], axis=1)
    inter = jnp.concatenate([top, bottom], axis=0) * (1.0 / node_total)
    frob2 = jnp.sum(jnp.sum(inter * inter, axis=1, keepdims=True), axis=0, keepdims=True)
    frob = jnp.sqrt(frob2)
    current = inter / frob
    row_id = lax.broadcasted_iota(jnp.int32, (256, 256), 0)
    col_id = lax.broadcasted_iota(jnp.int32, (256, 256), 1)
    identity = one_hot(row_id == col_id)
    square = dot3(current, current)
    tail = 1.6875 * identity - 0.5625 * current + 0.0625 * square
    factor_z = 2.25 * identity - 2.4375 * current + dot3(square, tail)
    return factor_z / jnp.sqrt(frob)


def at_offset(sizes, offset):
    n_gx, n_gy = sizes
    return (
        lax.rem(lax.axis_index("gx") + (offset[0] + n_gx), n_gx),
        lax.rem(lax.axis_index("gy") + (offset[1] + n_gy), n_gy),
    )


def remote(sizes, src, dst, send, recv, offset):
    return pltpu.make_async_remote_copy(
        src_ref=src, dst_ref=dst, send_sem=send, recv_sem=recv,
        device_id=at_offset(sizes, offset), device_id_type=pl.DeviceIdType.MESH,
    )


def greet(sizes, offsets):
    barrier = pltpu.get_barrier_semaphore()
    offsets = sorted({(dx % sizes[0], dy % sizes[1]) for dx, dy in offsets})
    for offset in offsets:
        pl.semaphore_signal(
            barrier, inc=1, device_id=at_offset(sizes, offset),
            device_id_type=pl.DeviceIdType.MESH,
        )
    return lambda: pl.semaphore_wait(barrier, len(offsets))


HALO_OFFSETS = [(dx, dy) for dx, dy, _, _, _ in MESSAGES]


def filter_phase(sizes, inputs, scratch, ready):
    (nodes_in, masses_in, cells_in, down_in, along_in) = inputs
    (nodes, masses, cells, down, along, padded, mass_pad, rim_matrix, inner_matrix, states,
     rim_rounded, inner_rounded, sums, sent_x, sent_y, sent_corner, got_x, got_y, got_corner,
     load_sems, send_sems, recv_sems) = scratch

    loads = [
        pltpu.make_async_copy(src, dst, load_sems.at[index])
        for index, (src, dst) in enumerate(
            [(down_in, down), (along_in, along), (cells_in, cells), (masses_in, masses),
             (nodes_in, nodes)]
        )
    ]
    for load in loads:
        load.start()
    loads[0].wait()
    loads[1].wait()

    lanes = lax.broadcasted_iota(jnp.int32, (ROWS, 216), 1)
    to_rows = [one_hot(lanes == down[:, c : c + 1]).astype(BF16) for c in range(2)]
    places = lax.broadcasted_iota(jnp.int32, (216, ROWS), 0)
    to_columns = [one_hot(places == along[c : c + 1, :]).astype(BF16) for c in range(2)]

    loads[2].wait()
    first = dot(to_rows[0], cells[0, 0, 0]).astype(BF16)
    second = dot(to_rows[1], cells[0, 0, 1]).astype(BF16)
    matrix = (dot(first, to_columns[0]) + dot(second, to_columns[1])).astype(BF16)
    rim_matrix[...] = matrix[:, :RIM]
    inner_matrix[...] = matrix[:, RIM:]

    loads[3].wait()
    mass_pad[...] = jnp.zeros(mass_pad.shape, F32)
    for x in range(6):
        high, rest = split(masses[x])
        low, least = split(masses[x] - high.astype(F32))
        mass_pad[8 * x : 8 * x + 6, 0:11] = high.astype(F32)
        mass_pad[8 * x : 8 * x + 6, 16:27] = low.astype(F32)
        mass_pad[8 * x : 8 * x + 6, 32:43] = least.astype(F32)
    pick = one_hot(lax.broadcasted_iota(jnp.int32, (ROWS, 48), 1) == down[:, 2:3]).astype(BF16)
    spread = dot(pick, mass_pad[...].astype(BF16))
    lane = lax.broadcasted_iota(jnp.int32, (ROWS, 128), 1)
    mass = jnp.sum(
        jnp.where(lane % 16 == down[:, 3:4], spread, 0.0), axis=1, keepdims=True
    )
    weight = mass * down[:, 4:5].astype(F32)
    scale1 = 1.0 / (HALF_SPAN * mass)
    shift = CENTER_SHIFT / HALF_SPAN

    loads[4].wait()
    for x in range(6):
        for z in range(11):
            for half in range(2):
                padded[half, 8 * (11 * x + z) : 8 * (11 * x + z) + 6] = nodes[
                    x, z, :, 128 * half : 128 * half + 128
                ].astype(F32)
    for (x, y), start in STARTS.items():
        for half in range(2):
            for low, skip in ((0, 0), (6, 40)):
                states[0, half, start + low : start + low + 6] = padded[
                    half, pl.ds(88 * x + skip + y, 6, stride=8)
                ]
    rim, inner = slice(0, RIM), slice(RIM, ROWS)
    for half in range(2):
        rim_rounded[half] = states[0, half, rim].astype(BF16)
        inner_rounded[half] = states[0, half, inner].astype(BF16)

    buffers = {"x": (sent_x, got_x), "y": (sent_y, got_y), "corner": (sent_corner, got_corner)}

    def moves_of(step, half):
        return [
            remote(
                sizes, buffers[kind][0].at[step, half, here], buffers[kind][1].at[step, half, there],
                send_sems.at[step, half, index], recv_sems.at[step, half, index], (dx, dy),
            )
            for index, (dx, dy, kind, here, there) in enumerate(MESSAGES)
        ]

    def advance(step, half, product, rows):
        if step == 0:
            return product * scale1[rows] - shift * states[0, half, rows]
        return (
            (2.0 * product) * scale1[rows]
            - (2.0 * shift) * states[step, half, rows]
            - states[step - 1, half, rows]
        )

    moves = {}

    def launch(step, half, ahead):
        product = ahead + dot(rim_matrix[rim], rim_rounded[half])
        sums[step, half] = product
        corners = [product[12 * i : 12 * i + 12] for i in range(4)]
        for i in range(4):
            sent_corner[step, half, i] = corners[i]
        sent_x[step, half, 0] = jnp.concatenate([corners[0], corners[2], product[48:96]], axis=0)
        sent_x[step, half, 1] = jnp.concatenate([corners[1], corners[3], product[96:144]], axis=0)
        sent_y[step, half, 0] = jnp.concatenate([product[0:24], product[144:192]], axis=0)
        sent_y[step, half, 1] = jnp.concatenate([product[24:48], product[192:240]], axis=0)
        if step == 0 and half == 0:
            ready()
        moves[step, half] = moves_of(step, half)
        for move in moves[step, half]:
            move.start()

    def inside(step, half):
        inner_next = advance(
            step,
            half,
            dot(rim_matrix[inner], rim_rounded[half])
            + dot(inner_matrix[inner], inner_rounded[half]),
            inner,
        )
        states[step + 1, half, inner] = inner_next
        if step == FILTER_DEG - 1:
            return inner_next
        inner_rounded[half] = inner_next.astype(BF16)
        return dot(inner_matrix[rim], inner_rounded[half])

    def finish(step, half):
        for move in moves[step, half]:
            move.wait_recv()
        own = sums[step, half]
        x0, x5 = got_x[step, half, 0], got_x[step, half, 1]
        y0, y5 = got_y[step, half, 0], got_y[step, half, 1]
        far = [got_corner[step, half, i] for i in range(4)]
        theirs = jnp.concatenate(
            [
                x0[0:12] + y0[0:12] + far[0],
                x5[0:12] + y0[12:24] + far[1],
                x0[12:24] + y5[0:12] + far[2],
                x5[12:24] + y5[12:24] + far[3],
                x0[24:72],
                x5[24:72],
                y0[24:72],
                y5[24:72],
            ],
            axis=0,
        )
        rim_next = advance(step, half, own + theirs, rim)
        states[step + 1, half, rim] = rim_next
        rim_rounded[half] = rim_next.astype(BF16)
        return rim_next

    for half in range(2):
        launch(0, half, dot(inner_matrix[rim], inner_rounded[half]))
    ahead = [inside(0, half) for half in range(2)]
    for step in range(FILTER_DEG - 1):
        for half in range(2):
            finish(step, half)
            launch(step + 1, half, ahead[half])
            ahead[half] = inside(step + 1, half)
    grams = gram(jnp.concatenate(ahead, axis=1), weight[inner])
    keep = lambda a: jnp.concatenate([a[0:24], a[48:96], a[144:192]], axis=0)
    rims = [keep(finish(FILTER_DEG - 1, half)) for half in range(2)]
    rim_grams = gram(jnp.concatenate(rims, axis=1), keep(weight[rim]))
    return tuple(a + b for a, b in zip(grams, rim_grams)), sum(moves.values(), [])


def whole_rows(states):
    return jnp.concatenate([states[FILTER_DEG, 0], states[FILTER_DEG, 1]], axis=1)


def rotate_phase(filtered, factor, padded, out):
    result = dot3(filtered, factor)
    for (x, y), start in STARTS.items():
        for half in range(2):
            lanes = slice(128 * half, 128 * half + 128)
            padded[half, pl.ds(88 * x + y, 6, stride=8)] = result[start : start + 6, lanes]
            padded[half, pl.ds(88 * x + 48 + y, 5, stride=8)] = result[
                start + 7 : start + 12, lanes
            ]
    for x in range(6):
        for z in range(11):
            low = 8 * (11 * x + z)
            out[x, z] = jnp.concatenate(
                [padded[0, low : low + 6], padded[1, low : low + 6]], axis=1
            ).astype(BF16)


def fused_kernel(sizes, node_total, *refs):
    inputs, out, scratch, extra = refs[:5], refs[5], refs[6:28], refs[28:]
    (own, row_in, part, column_in, whole,
     row_send, row_recv, col_send, col_recv, all_send, all_recv) = extra
    n_gx, n_gy = sizes
    my_y = lax.axis_index("gy")
    ready = greet(
        sizes,
        HALO_OFFSETS + [(0, d) for d in range(1, n_gy)] + [(d, 0) for d in range(1, n_gx)],
    )
    grams, moves = filter_phase(sizes, inputs, scratch, ready)
    pieces, height = own.shape[0], own.shape[2] - 1
    packed, diagonal = pack(grams)
    row_moves, col_moves, all_moves = [], [], []
    for p in range(pieces):
        for index in range(n_gy):
            low = (index * pieces + p) * height
            own[p, index, 0:height] = packed[low : low + height]
            own[p, index, height : height + 1] = diagonal
        row_moves.append([
            remote(sizes, own.at[p, lax.rem(my_y + d, n_gy)], row_in.at[p, d - 1],
                   row_send.at[p, d - 1], row_recv.at[p, d - 1], (0, d))
            for d in range(1, n_gy)
        ])
        for move in row_moves[p]:
            move.start()
        col_moves.append([
            remote(sizes, part.at[p], column_in.at[p, d - 1],
                   col_send.at[p, d - 1], col_recv.at[p, d - 1], (d, 0))
            for d in range(1, n_gx)
        ])
        all_moves.append([
            remote(sizes, whole.at[p, my_y], whole.at[p, my_y],
                   all_send.at[p, d - 1], all_recv.at[p, d - 1], (0, d))
            for d in range(1, n_gy)
        ])

    def second(p):
        for move in row_moves[p]:
            move.wait_recv()
        total = own[p, my_y]
        for d in range(1, n_gy):
            total = total + row_in[p, d - 1]
        part[p] = total
        for move in col_moves[p]:
            move.start()

    def third(p):
        for move in col_moves[p]:
            move.wait_recv()
        total = part[p]
        for d in range(1, n_gx):
            total = total + column_in[p, d - 1]
        whole[p, my_y] = total
        for move in all_moves[p]:
            move.start()

    for p in range(pieces):
        second(p)
        if p >= 1:
            third(p - 1)
    third(pieces - 1)
    for p in range(pieces):
        for move in all_moves[p]:
            move.wait_recv()
    packed = jnp.concatenate(
        [whole[p, index, 0:height] for index in range(n_gy) for p in range(pieces)], axis=0
    )
    stacked = unpack(packed, whole[0, 0, height : height + 1])
    factor = inverse_root(stacked, node_total)
    rotate_phase(whole_rows(scratch[9]), factor, scratch[5], out)
    for move in moves + sum(row_moves + col_moves + all_moves, []):
        move.wait_send()


def filter_kernel(sizes, *refs):
    inputs, filtered, stacked, scratch = refs[:5], refs[5], refs[6], refs[7:]
    grams, moves = filter_phase(sizes, inputs, scratch, greet(sizes, HALO_OFFSETS))
    stacked[...] = jnp.concatenate(grams, axis=0)
    filtered[...] = whole_rows(scratch[9])
    for move in moves:
        move.wait_send()


def rotate_kernel(node_total, filtered, stacked, out, padded):
    rotate_phase(filtered[...], inverse_root(stacked[...], node_total), padded, out)


def body(orbitals, masses, cell_matrices):
    n_gx, n_gy = lax.axis_size("gx"), lax.axis_size("gy")
    sizes = (n_gx, n_gy)
    assert orbitals.shape == (6, 6, 11, 256) and cell_matrices.shape == (1, 1, 2, 216, 216)
    node_total = 5 * n_gx * 5 * n_gy * 11
    nodes = jnp.transpose(orbitals, (0, 2, 1, 3))
    down, along = tables()
    arguments = (nodes, masses, cell_matrices, jnp.asarray(down), jnp.asarray(along))
    arguments = tuple(pltpu.with_memory_space_constraint(a, pltpu.HBM) for a in arguments)
    vmem = pl.BlockSpec(memory_space=pltpu.VMEM)
    hbm = pl.BlockSpec(memory_space=pltpu.MemorySpace.HBM)
    filter_scratch = [
        pltpu.VMEM(nodes.shape, BF16),
        pltpu.VMEM(masses.shape, F32),
        pltpu.VMEM(cell_matrices.shape, BF16),
        pltpu.VMEM(down.shape, jnp.int32),
        pltpu.VMEM(along.shape, jnp.int32),
        pltpu.VMEM((2, 528, 128), F32),
        pltpu.VMEM((48, 128), F32),
        pltpu.VMEM((ROWS, RIM), BF16),
        pltpu.VMEM((ROWS, INNER), BF16),
        pltpu.VMEM((FILTER_DEG + 1, 2, ROWS, 128), F32),
        pltpu.VMEM((2, RIM, 128), BF16),
        pltpu.VMEM((2, INNER, 128), BF16),
        pltpu.VMEM((FILTER_DEG, 2, RIM, 128), F32),
    ]
    filter_scratch += [
        pltpu.VMEM((FILTER_DEG, 2) + shape + (128,), F32)
        for shape in ((2, 72), (2, 72), (4, 12)) * 2
    ]
    filter_scratch += [
        pltpu.SemaphoreType.DMA((5,)),
        pltpu.SemaphoreType.DMA((FILTER_DEG, 2, len(MESSAGES))),
        pltpu.SemaphoreType.DMA((FILTER_DEG, 2, len(MESSAGES))),
    ]
    params = pltpu.CompilerParams(
        collective_id=0, has_side_effects=True, vmem_limit_bytes=VMEM_BYTES
    )
    if 256 % (8 * PIECES * n_gy) == 0:
        height = 256 // n_gy // PIECES + 1
        result = pl.pallas_call(
            functools.partial(fused_kernel, sizes, node_total),
            out_shape=pltpu.VMEM(nodes.shape, BF16),
            in_specs=[hbm] * 5,
            out_specs=vmem,
            scratch_shapes=filter_scratch
            + [
                pltpu.VMEM((PIECES, n_gy, height, 128), F32),
                pltpu.VMEM((PIECES, n_gy - 1, height, 128), F32),
                pltpu.VMEM((PIECES, height, 128), F32),
                pltpu.VMEM((PIECES, n_gx - 1, height, 128), F32),
                pltpu.VMEM((PIECES, n_gy, height, 128), F32),
            ]
            + [pltpu.SemaphoreType.DMA((PIECES, n - 1)) for n in (n_gy, n_gy, n_gx, n_gx, n_gy, n_gy)],
            compiler_params=params,
        )(*arguments)
    else:
        filtered, stacked = pl.pallas_call(
            functools.partial(filter_kernel, sizes),
            out_shape=[
                jax.ShapeDtypeStruct((ROWS, 256), F32),
                jax.ShapeDtypeStruct((384, 128), F32),
            ],
            in_specs=[hbm] * 5,
            out_specs=[vmem] * 2,
            scratch_shapes=filter_scratch,
            compiler_params=params,
        )(*arguments)
        stacked = lax.psum(stacked, ("gx", "gy"))
        result = pl.pallas_call(
            functools.partial(rotate_kernel, node_total),
            out_shape=jax.ShapeDtypeStruct(nodes.shape, BF16),
            in_specs=[vmem] * 2,
            out_specs=vmem,
            scratch_shapes=[pltpu.VMEM((2, 528, 128), F32)],
            compiler_params=pltpu.CompilerParams(vmem_limit_bytes=VMEM_BYTES),
        )(filtered, stacked)
    return jnp.transpose(result, (0, 2, 1, 3))


def solution(mesh):
    return jax.shard_map(
        body,
        mesh=mesh,
        in_specs=(P("gx", "gy", None, None), P("gx", "gy", None), P("gx", "gy", None, None, None)),
        out_specs=P("gx", "gy", None, None),
        check_vma=False,
    )
```

```python
import functools

import jax
import jax.numpy as jnp
import numpy as np
from jax import lax
from jax.experimental import pallas as pl
from jax.experimental.pallas import tpu as pltpu
from jax.sharding import PartitionSpec as P

FILTER_DEG = 3
CENTER_SHIFT = 12.0
HALF_SPAN = 12.0

RIM = 240
ROWS = 432
INNER = ROWS - RIM
CORNERS = 48
PIECES = 1
VMEM_BYTES = 24 << 20
BF16 = jnp.bfloat16
F32 = jnp.float32

MESSAGES = (
    (-1, -1, "corner", 0, 3),
    (1, -1, "corner", 1, 2),
    (-1, 1, "corner", 2, 1),
    (1, 1, "corner", 3, 0),
    (-1, 0, "x", 0, 1),
    (1, 0, "x", 1, 0),
    (0, -1, "y", 0, 1),
    (0, 1, "y", 1, 0),
)


def column_starts():
    starts = {(0, 0): 0, (5, 0): 12, (0, 5): 24, (5, 5): 36}
    for i in range(4):
        starts[(0, i + 1)] = 48 + 12 * i
        starts[(5, i + 1)] = 96 + 12 * i
        starts[(i + 1, 0)] = 144 + 12 * i
        starts[(i + 1, 5)] = 192 + 12 * i
    for i in range(4):
        for j in range(4):
            starts[(i + 1, j + 1)] = RIM + 12 * (4 * i + j)
    return starts


STARTS = column_starts()
FIRST = (3, 5, 7)
OWNED = (slice(0, 12), slice(48, 96), slice(144, 192))
OTHERS = (slice(12, 48), slice(96, 144), slice(192, 240))


def tables():
    down = np.zeros((ROWS, 128), np.int32)
    along = np.full((8, ROWS), -1, np.int32)
    for (x, y), start in STARTS.items():
        for half in range(2):
            for k in range(6):
                row, z = start + 6 * half + k, 5 * half + k
                for cell in range(2):
                    inside = 0 <= z - 5 * cell <= 5
                    down[row, cell] = (x * 6 + y) * 6 + z - 5 * cell if inside else -1
                down[row, 2], down[row, 3] = 8 * x + y, z
                down[row, 4] = int(x < 5 and y < 5 and not (half == 1 and k == 0))
                along[half, row] = (x * 6 + y) * 6 + k
    return down, along


def dot(a, b):
    return jnp.dot(a, b, preferred_element_type=F32)


def dot_rows(a, b):
    return lax.dot_general(a, b, (((0,), (0,)), ((), ())), preferred_element_type=F32)


def split(a):
    high = a.astype(BF16)
    return high, (a - high.astype(F32)).astype(BF16)


def dot3(a, b):
    a_high, a_low = split(a)
    b_high, b_low = split(b)
    return dot(a_high, b_high) + (dot(a_high, b_low) + dot(a_low, b_high))


def one_hot(condition):
    return jnp.where(condition, 1.0, 0.0).astype(F32)


def gram(rows, weight):
    a_high, a_low = split(rows * weight)
    b_high, b_low = split(rows)

    def part(lanes, columns):
        return dot_rows(a_high[:, lanes], b_high[:, columns]) + (
            dot_rows(a_high[:, lanes], b_low[:, columns])
            + dot_rows(a_low[:, lanes], b_high[:, columns])
        )

    top = part(slice(0, 128), slice(0, 256))
    return top[:, :128], top[:, 128:], part(slice(128, 256), slice(128, 256))


def block_ids():
    return (
        lax.broadcasted_iota(jnp.int32, (128, 128), 0),
        lax.broadcasted_iota(jnp.int32, (128, 128), 1),
    )


def pack(grams):
    s00, s01, s11 = grams
    row, col = block_ids()
    diagonal = jnp.sum(jnp.where(row == col, s11, 0.0), axis=0, keepdims=True)
    return jnp.concatenate([s01, jnp.where(row <= col, s00, s11)], axis=0), diagonal


def unpack(packed, diagonal):
    s01, both = packed[0:128], packed[128:256]
    row, col = block_ids()
    upper = jnp.where(row <= col, both, 0.0)
    lower = jnp.where(row > col, both, 0.0)
    s00 = upper + jnp.where(row < col, both, 0.0).T
    s11 = lower + lower.T + jnp.where(row == col, diagonal, 0.0)
    return jnp.concatenate([s00, s01, s11], axis=0)


def inverse_root(stacked, node_total):
    s00, s01, s11 = stacked[0:128], stacked[128:256], stacked[256:384]
    top = jnp.concatenate([s00, s01], axis=1)
    bottom = jnp.concatenate([s01.T, s11], axis=1)
    inter = jnp.concatenate([top, bottom], axis=0) * (1.0 / node_total)
    frob2 = jnp.sum(jnp.sum(inter * inter, axis=1, keepdims=True), axis=0, keepdims=True)
    frob = jnp.sqrt(frob2)
    current = inter / frob
    row_id = lax.broadcasted_iota(jnp.int32, (256, 256), 0)
    col_id = lax.broadcasted_iota(jnp.int32, (256, 256), 1)
    identity = one_hot(row_id == col_id)
    square = dot3(current, current)
    tail = 1.6875 * identity - 0.5625 * current + 0.0625 * square
    factor_z = 2.25 * identity - 2.4375 * current + dot3(square, tail)
    return factor_z / jnp.sqrt(frob)


def at_offset(sizes, offset):
    n_gx, n_gy = sizes
    return (
        lax.rem(lax.axis_index("gx") + (offset[0] + n_gx), n_gx),
        lax.rem(lax.axis_index("gy") + (offset[1] + n_gy), n_gy),
    )


def remote(sizes, src, dst, send, recv, offset):
    return pltpu.make_async_remote_copy(
        src_ref=src, dst_ref=dst, send_sem=send, recv_sem=recv,
        device_id=at_offset(sizes, offset), device_id_type=pl.DeviceIdType.MESH,
    )


def greet(sizes, offsets):
    barrier = pltpu.get_barrier_semaphore()
    offsets = sorted({(dx % sizes[0], dy % sizes[1]) for dx, dy in offsets})
    for offset in offsets:
        pl.semaphore_signal(
            barrier, inc=1, device_id=at_offset(sizes, offset),
            device_id_type=pl.DeviceIdType.MESH,
        )
    return lambda: pl.semaphore_wait(barrier, len(offsets))


HALO_OFFSETS = [(dx, dy) for dx, dy, _, _, _ in MESSAGES]


def filter_phase(sizes, inputs, scratch, ready):
    (nodes_in, masses_in, cells_in, down_in, along_in) = inputs
    (nodes, masses, cells, down, along, padded, mass_pad, rim_matrix, inner_matrix, states,
     rim_rounded, inner_rounded, sums, sent_x, sent_y, sent_corner, got_x, got_y, got_corner,
     load_sems, send_sems, recv_sems) = scratch

    loads = [
        pltpu.make_async_copy(src, dst, load_sems.at[index])
        for index, (src, dst) in enumerate(
            [(down_in, down), (along_in, along), (cells_in, cells), (masses_in, masses),
             (nodes_in, nodes)]
        )
    ]
    for load in loads:
        load.start()
    loads[0].wait()
    loads[1].wait()

    lanes = lax.broadcasted_iota(jnp.int32, (ROWS, 216), 1)
    to_rows = [one_hot(lanes == down[:, c : c + 1]).astype(BF16) for c in range(2)]
    places = lax.broadcasted_iota(jnp.int32, (216, ROWS), 0)
    to_columns = [one_hot(places == along[c : c + 1, :]).astype(BF16) for c in range(2)]

    loads[2].wait()
    first = dot(to_rows[0], cells[0, 0, 0]).astype(BF16)
    second = dot(to_rows[1], cells[0, 0, 1]).astype(BF16)
    matrix = (dot(first, to_columns[0]) + dot(second, to_columns[1])).astype(BF16)
    rim_matrix[...] = matrix[:, :RIM]
    inner_matrix[...] = matrix[:, RIM:]

    loads[3].wait()
    mass_pad[...] = jnp.zeros(mass_pad.shape, F32)
    for x in range(6):
        high, rest = split(masses[x])
        low, least = split(masses[x] - high.astype(F32))
        mass_pad[8 * x : 8 * x + 6, 0:11] = high.astype(F32)
        mass_pad[8 * x : 8 * x + 6, 16:27] = low.astype(F32)
        mass_pad[8 * x : 8 * x + 6, 32:43] = least.astype(F32)
    pick = one_hot(lax.broadcasted_iota(jnp.int32, (ROWS, 48), 1) == down[:, 2:3]).astype(BF16)
    spread = dot(pick, mass_pad[...].astype(BF16))
    lane = lax.broadcasted_iota(jnp.int32, (ROWS, 128), 1)
    mass = jnp.sum(
        jnp.where(lane % 16 == down[:, 3:4], spread, 0.0), axis=1, keepdims=True
    )
    weight = mass * down[:, 4:5].astype(F32)
    scale1 = 1.0 / (HALF_SPAN * mass)
    shift = CENTER_SHIFT / HALF_SPAN

    loads[4].wait()
    for x in range(6):
        for z in range(11):
            for half in range(2):
                padded[half, 8 * (11 * x + z) : 8 * (11 * x + z) + 6] = nodes[
                    x, z, :, 128 * half : 128 * half + 128
                ].astype(F32)
    for (x, y), start in STARTS.items():
        for half in range(2):
            for low, skip in ((0, 0), (6, 40)):
                states[0, half, start + low : start + low + 6] = padded[
                    half, pl.ds(88 * x + skip + y, 6, stride=8)
                ]
    rim, inner = slice(0, RIM), slice(RIM, ROWS)
    for half in range(2):
        rim_rounded[half] = states[0, half, rim].astype(BF16)
        inner_rounded[half] = states[0, half, inner].astype(BF16)

    buffers = {"x": (sent_x, got_x), "y": (sent_y, got_y), "corner": (sent_corner, got_corner)}

    def moves_of(step, half):
        return [
            remote(
                sizes, buffers[kind][0].at[step, half, here], buffers[kind][1].at[step, half, there],
                send_sems.at[step, half, index], recv_sems.at[step, half, index], (dx, dy),
            )
            for index, (dx, dy, kind, here, there) in enumerate(MESSAGES)
        ]

    def advance(step, half, product, rows):
        if step == 0:
            return product * scale1[rows] - shift * states[0, half, rows]
        return (
            (2.0 * product) * scale1[rows]
            - (2.0 * shift) * states[step, half, rows]
            - states[step - 1, half, rows]
        )

    moves = {}

    def launch(step, half, ahead):
        product = ahead + dot(rim_matrix[rim], rim_rounded[half])
        sums[step, half] = product
        corners = [product[12 * i : 12 * i + 12] for i in range(4)]
        for i in range(4):
            sent_corner[step, half, i] = corners[i]
        sent_x[step, half, 0] = jnp.concatenate([corners[0], corners[2], product[48:96]], axis=0)
        sent_x[step, half, 1] = jnp.concatenate([corners[1], corners[3], product[96:144]], axis=0)
        sent_y[step, half, 0] = jnp.concatenate([product[0:24], product[144:192]], axis=0)
        sent_y[step, half, 1] = jnp.concatenate([product[24:48], product[192:240]], axis=0)
        if step == 0 and half == 0:
            ready()
        moves[step, half] = moves_of(step, half)
        for index, move in enumerate(moves[step, half]):
            if step < FILTER_DEG - 1 or index in FIRST:
                move.start()

    def inside(step, half):
        inner_next = advance(
            step,
            half,
            dot(rim_matrix[inner], rim_rounded[half])
            + dot(inner_matrix[inner], inner_rounded[half]),
            inner,
        )
        states[step + 1, half, inner] = inner_next
        if step == FILTER_DEG - 1:
            return inner_next
        inner_rounded[half] = inner_next.astype(BF16)
        return dot(inner_matrix[rim], inner_rounded[half])

    def finish(step, half):
        for move in moves[step, half]:
            move.wait_recv()
        own = sums[step, half]
        x0, x5 = got_x[step, half, 0], got_x[step, half, 1]
        y0, y5 = got_y[step, half, 0], got_y[step, half, 1]
        far = [got_corner[step, half, i] for i in range(4)]
        theirs = jnp.concatenate(
            [
                x0[0:12] + y0[0:12] + far[0],
                x5[0:12] + y0[12:24] + far[1],
                x0[12:24] + y5[0:12] + far[2],
                x5[12:24] + y5[12:24] + far[3],
                x0[24:72],
                x5[24:72],
                y0[24:72],
                y5[24:72],
            ],
            axis=0,
        )
        rim_next = advance(step, half, own + theirs, rim)
        states[step + 1, half, rim] = rim_next
        rim_rounded[half] = rim_next.astype(BF16)
        return rim_next

    for half in range(2):
        launch(0, half, dot(inner_matrix[rim], inner_rounded[half]))
    ahead = [inside(0, half) for half in range(2)]
    for step in range(FILTER_DEG - 1):
        for half in range(2):
            finish(step, half)
            launch(step + 1, half, ahead[half])
            ahead[half] = inside(step + 1, half)
    grams = gram(jnp.concatenate(ahead, axis=1), weight[inner])
    last = FILTER_DEG - 1

    def set_last(half, groups, theirs):
        values = []
        for rows, their in zip(groups, theirs):
            values.append(advance(last, half, sums[last, half, rows] + their, rows))
            states[last + 1, half, rows] = values[-1]
        return jnp.concatenate(values, axis=0)

    def finish_owned(half):
        for index in FIRST:
            moves[last, half][index].wait_recv()
        x0, y0 = got_x[last, half, 0], got_y[last, half, 0]
        corner = x0[0:12] + y0[0:12] + got_corner[last, half, 0]
        return set_last(half, OWNED, (corner, x0[24:72], y0[24:72]))

    def start_others(indices):
        for half in range(2):
            for index in indices:
                moves[last, half][index].start()

    def finish_others():
        for half in range(2):
            for index, move in enumerate(moves[last, half]):
                if index not in FIRST:
                    move.wait_recv()
            x0, x5 = got_x[last, half, 0], got_x[last, half, 1]
            y0, y5 = got_y[last, half, 0], got_y[last, half, 1]
            corners = jnp.concatenate(
                [
                    x5[0:12] + y0[12:24] + got_corner[last, half, 1],
                    x0[12:24] + y5[0:12] + got_corner[last, half, 2],
                    x5[12:24] + y5[12:24] + got_corner[last, half, 3],
                ],
                axis=0,
            )
            set_last(half, OTHERS, (corners, x5[24:72], y5[24:72]))

    rims = [finish_owned(half) for half in range(2)]
    rim_weight = jnp.concatenate([weight[rows] for rows in OWNED], axis=0)
    rim_grams = gram(jnp.concatenate(rims, axis=1), rim_weight)
    grams = tuple(a + b for a, b in zip(grams, rim_grams))
    return grams, sum(moves.values(), []), start_others, finish_others


def whole_rows(states):
    return jnp.concatenate([states[FILTER_DEG, 0], states[FILTER_DEG, 1]], axis=1)


def rotate_phase(filtered, factor, padded, out):
    result = dot3(filtered, factor)
    for (x, y), start in STARTS.items():
        for half in range(2):
            lanes = slice(128 * half, 128 * half + 128)
            padded[half, pl.ds(88 * x + y, 6, stride=8)] = result[start : start + 6, lanes]
            padded[half, pl.ds(88 * x + 48 + y, 5, stride=8)] = result[
                start + 7 : start + 12, lanes
            ]
    for x in range(6):
        for z in range(11):
            low = 8 * (11 * x + z)
            out[x, z] = jnp.concatenate(
                [padded[0, low : low + 6], padded[1, low : low + 6]], axis=1
            ).astype(BF16)


def fused_kernel(sizes, node_total, *refs):
    inputs, out, scratch, extra = refs[:5], refs[5], refs[6:28], refs[28:]
    (own, row_in, part, column_in, whole,
     row_send, row_recv, col_send, col_recv, all_send, all_recv) = extra
    n_gx, n_gy = sizes
    my_y = lax.axis_index("gy")
    ready = greet(
        sizes,
        HALO_OFFSETS + [(0, d) for d in range(1, n_gy)] + [(d, 0) for d in range(1, n_gx)],
    )
    grams, moves, start_others, finish_others = filter_phase(sizes, inputs, scratch, ready)
    pieces, height = own.shape[0], own.shape[2] - 1
    packed, diagonal = pack(grams)
    row_moves, col_moves, all_moves = [], [], []
    for p in range(pieces):
        for index in range(n_gy):
            low = (index * pieces + p) * height
            own[p, index, 0:height] = packed[low : low + height]
            own[p, index, height : height + 1] = diagonal
        row_moves.append([
            remote(sizes, own.at[p, lax.rem(my_y + d, n_gy)], row_in.at[p, d - 1],
                   row_send.at[p, d - 1], row_recv.at[p, d - 1], (0, d))
            for d in range(1, n_gy)
        ])
        for move in row_moves[p]:
            move.start()
        if p == pieces - 1:
            start_others((0, 1, 2, 4))
        col_moves.append([
            remote(sizes, part.at[p], column_in.at[p, d - 1],
                   col_send.at[p, d - 1], col_recv.at[p, d - 1], (d, 0))
            for d in range(1, n_gx)
        ])
        all_moves.append([
            remote(sizes, whole.at[p, my_y], whole.at[p, my_y],
                   all_send.at[p, d - 1], all_recv.at[p, d - 1], (0, d))
            for d in range(1, n_gy)
        ])

    def second(p):
        for move in row_moves[p]:
            move.wait_recv()
        total = own[p, my_y]
        for d in range(1, n_gy):
            total = total + row_in[p, d - 1]
        part[p] = total
        for move in col_moves[p]:
            move.start()

    def third(p):
        for move in col_moves[p]:
            move.wait_recv()
        total = part[p]
        for d in range(1, n_gx):
            total = total + column_in[p, d - 1]
        whole[p, my_y] = total
        for move in all_moves[p]:
            move.start()

    for p in range(pieces):
        second(p)
        if p >= 1:
            third(p - 1)
    start_others((6,))
    third(pieces - 1)
    finish_others()
    for p in range(pieces):
        for move in all_moves[p]:
            move.wait_recv()
    packed = jnp.concatenate(
        [whole[p, index, 0:height] for index in range(n_gy) for p in range(pieces)], axis=0
    )
    stacked = unpack(packed, whole[0, 0, height : height + 1])
    factor = inverse_root(stacked, node_total)
    rotate_phase(whole_rows(scratch[9]), factor, scratch[5], out)
    for move in moves + sum(row_moves + col_moves + all_moves, []):
        move.wait_send()


def filter_kernel(sizes, *refs):
    inputs, filtered, stacked, scratch = refs[:5], refs[5], refs[6], refs[7:]
    grams, moves, start_others, finish_others = filter_phase(
        sizes, inputs, scratch, greet(sizes, HALO_OFFSETS)
    )
    start_others((0, 1, 2, 4, 6))
    finish_others()
    stacked[...] = jnp.concatenate(grams, axis=0)
    filtered[...] = whole_rows(scratch[9])
    for move in moves:
        move.wait_send()


def rotate_kernel(node_total, filtered, stacked, out, padded):
    rotate_phase(filtered[...], inverse_root(stacked[...], node_total), padded, out)


def body(orbitals, masses, cell_matrices):
    n_gx, n_gy = lax.axis_size("gx"), lax.axis_size("gy")
    sizes = (n_gx, n_gy)
    assert orbitals.shape == (6, 6, 11, 256) and cell_matrices.shape == (1, 1, 2, 216, 216)
    node_total = 5 * n_gx * 5 * n_gy * 11
    nodes = jnp.transpose(orbitals, (0, 2, 1, 3))
    down, along = tables()
    arguments = (nodes, masses, cell_matrices, jnp.asarray(down), jnp.asarray(along))
    arguments = tuple(pltpu.with_memory_space_constraint(a, pltpu.HBM) for a in arguments)
    vmem = pl.BlockSpec(memory_space=pltpu.VMEM)
    hbm = pl.BlockSpec(memory_space=pltpu.MemorySpace.HBM)
    filter_scratch = [
        pltpu.VMEM(nodes.shape, BF16),
        pltpu.VMEM(masses.shape, F32),
        pltpu.VMEM(cell_matrices.shape, BF16),
        pltpu.VMEM(down.shape, jnp.int32),
        pltpu.VMEM(along.shape, jnp.int32),
        pltpu.VMEM((2, 528, 128), F32),
        pltpu.VMEM((48, 128), F32),
        pltpu.VMEM((ROWS, RIM), BF16),
        pltpu.VMEM((ROWS, INNER), BF16),
        pltpu.VMEM((FILTER_DEG + 1, 2, ROWS, 128), F32),
        pltpu.VMEM((2, RIM, 128), BF16),
        pltpu.VMEM((2, INNER, 128), BF16),
        pltpu.VMEM((FILTER_DEG, 2, RIM, 128), F32),
    ]
    filter_scratch += [
        pltpu.VMEM((FILTER_DEG, 2) + shape + (128,), F32)
        for shape in ((2, 72), (2, 72), (4, 12)) * 2
    ]
    filter_scratch += [
        pltpu.SemaphoreType.DMA((5,)),
        pltpu.SemaphoreType.DMA((FILTER_DEG, 2, len(MESSAGES))),
        pltpu.SemaphoreType.DMA((FILTER_DEG, 2, len(MESSAGES))),
    ]
    params = pltpu.CompilerParams(
        collective_id=0, has_side_effects=True, vmem_limit_bytes=VMEM_BYTES
    )
    if 256 % (8 * PIECES * n_gy) == 0:
        height = 256 // n_gy // PIECES + 1
        result = pl.pallas_call(
            functools.partial(fused_kernel, sizes, node_total),
            out_shape=pltpu.VMEM(nodes.shape, BF16),
            in_specs=[hbm] * 5,
            out_specs=vmem,
            scratch_shapes=filter_scratch
            + [
                pltpu.VMEM((PIECES, n_gy, height, 128), F32),
                pltpu.VMEM((PIECES, n_gy - 1, height, 128), F32),
                pltpu.VMEM((PIECES, height, 128), F32),
                pltpu.VMEM((PIECES, n_gx - 1, height, 128), F32),
                pltpu.VMEM((PIECES, n_gy, height, 128), F32),
            ]
            + [pltpu.SemaphoreType.DMA((PIECES, n - 1)) for n in (n_gy, n_gy, n_gx, n_gx, n_gy, n_gy)],
            compiler_params=params,
        )(*arguments)
    else:
        filtered, stacked = pl.pallas_call(
            functools.partial(filter_kernel, sizes),
            out_shape=[
                jax.ShapeDtypeStruct((ROWS, 256), F32),
                jax.ShapeDtypeStruct((384, 128), F32),
            ],
            in_specs=[hbm] * 5,
            out_specs=[vmem] * 2,
            scratch_shapes=filter_scratch,
            compiler_params=params,
        )(*arguments)
        stacked = lax.psum(stacked, ("gx", "gy"))
        result = pl.pallas_call(
            functools.partial(rotate_kernel, node_total),
            out_shape=jax.ShapeDtypeStruct(nodes.shape, BF16),
            in_specs=[vmem] * 2,
            out_specs=vmem,
            scratch_shapes=[pltpu.VMEM((2, 528, 128), F32)],
            compiler_params=pltpu.CompilerParams(vmem_limit_bytes=VMEM_BYTES),
        )(filtered, stacked)
    return jnp.transpose(result, (0, 2, 1, 3))


def solution(mesh):
    return jax.shard_map(
        body,
        mesh=mesh,
        in_specs=(P("gx", "gy", None, None), P("gx", "gy", None), P("gx", "gy", None, None, None)),
        out_specs=P("gx", "gy", None, None),
        check_vma=False,
    )
```

```python
import functools

import jax
import jax.numpy as jnp
import numpy as np
from jax import lax
from jax.experimental import pallas as pl
from jax.experimental.pallas import tpu as pltpu
from jax.sharding import PartitionSpec as P

FILTER_DEG = 3
CENTER_SHIFT = 12.0
HALF_SPAN = 12.0

RIM = 240
ROWS = 432
INNER = ROWS - RIM
CORNERS = 48
PIECES = 1
VMEM_BYTES = 24 << 20
BF16 = jnp.bfloat16
F32 = jnp.float32

MESSAGES = (
    (-1, -1, "corner", 0, 3),
    (1, -1, "corner", 1, 2),
    (-1, 1, "corner", 2, 1),
    (1, 1, "corner", 3, 0),
    (-1, 0, "x", 0, 1),
    (1, 0, "x", 1, 0),
    (0, -1, "y", 0, 1),
    (0, 1, "y", 1, 0),
)


def column_starts():
    starts = {(0, 0): 0, (5, 0): 12, (0, 5): 24, (5, 5): 36}
    for i in range(4):
        starts[(0, i + 1)] = 48 + 12 * i
        starts[(5, i + 1)] = 96 + 12 * i
        starts[(i + 1, 0)] = 144 + 12 * i
        starts[(i + 1, 5)] = 192 + 12 * i
    for i in range(4):
        for j in range(4):
            starts[(i + 1, j + 1)] = RIM + 12 * (4 * i + j)
    return starts


STARTS = column_starts()
FIRST = (3, 5, 7)
OWNED = (slice(0, 12), slice(48, 96), slice(144, 192))
OTHERS = (slice(12, 48), slice(96, 144), slice(192, 240))


def tables():
    down = np.zeros((ROWS, 128), np.int32)
    along = np.full((8, ROWS), -1, np.int32)
    for (x, y), start in STARTS.items():
        for half in range(2):
            for k in range(6):
                row, z = start + 6 * half + k, 5 * half + k
                for cell in range(2):
                    inside = 0 <= z - 5 * cell <= 5
                    down[row, cell] = (x * 6 + y) * 6 + z - 5 * cell if inside else -1
                down[row, 2], down[row, 3] = 8 * x + y, z
                down[row, 4] = int(x < 5 and y < 5 and not (half == 1 and k == 0))
                along[half, row] = (x * 6 + y) * 6 + k
    return down, along


def dot(a, b):
    return jnp.dot(a, b, preferred_element_type=F32)


def dot_rows(a, b):
    return lax.dot_general(a, b, (((0,), (0,)), ((), ())), preferred_element_type=F32)


def split(a):
    high = a.astype(BF16)
    return high, (a - high.astype(F32)).astype(BF16)


def dot3(a, b):
    a_high, a_low = split(a)
    b_high, b_low = split(b)
    return dot(a_high, b_high) + (dot(a_high, b_low) + dot(a_low, b_high))


def one_hot(condition):
    return jnp.where(condition, 1.0, 0.0).astype(F32)


def gram(rows, weight):
    a_high, a_low = split(rows * weight)
    b_high, b_low = split(rows)

    def part(lanes, columns):
        return dot_rows(a_high[:, lanes], b_high[:, columns]) + (
            dot_rows(a_high[:, lanes], b_low[:, columns])
            + dot_rows(a_low[:, lanes], b_high[:, columns])
        )

    top = part(slice(0, 128), slice(0, 256))
    return top[:, :128], top[:, 128:], part(slice(128, 256), slice(128, 256))


def block_ids():
    return (
        lax.broadcasted_iota(jnp.int32, (128, 128), 0),
        lax.broadcasted_iota(jnp.int32, (128, 128), 1),
    )


def pack(grams):
    s00, s01, s11 = grams
    row, col = block_ids()
    diagonal = jnp.sum(jnp.where(row == col, s11, 0.0), axis=0, keepdims=True)
    return jnp.concatenate([s01, jnp.where(row <= col, s00, s11)], axis=0), diagonal


def unpack(packed, diagonal):
    s01, both = packed[0:128], packed[128:256]
    turned = both.T
    row, col = block_ids()
    s00 = jnp.where(row <= col, both, turned)
    s11 = jnp.where(row > col, both, jnp.where(row < col, turned, diagonal))
    return whole_gram(s00, s01, s11)


def whole_gram(s00, s01, s11):
    top = jnp.concatenate([s00, s01], axis=1)
    bottom = jnp.concatenate([s01.T, s11], axis=1)
    return jnp.concatenate([top, bottom], axis=0)


def inverse_root(gram_sum, node_total):
    inter = gram_sum * (1.0 / node_total)
    inter2 = dot3(inter, inter)
    frob2 = jnp.sum(jnp.sum(inter * inter, axis=0, keepdims=True), axis=1, keepdims=True)
    frob = jnp.sqrt(frob2)
    over = 1.0 / frob
    current = inter * over
    square = (inter2 * over) * over
    row_id = lax.broadcasted_iota(jnp.int32, (256, 256), 0)
    col_id = lax.broadcasted_iota(jnp.int32, (256, 256), 1)
    identity = one_hot(row_id == col_id)
    tail = 1.6875 * identity - 0.5625 * current + 0.0625 * square
    factor_z = 2.25 * identity - 2.4375 * current + dot3(square, tail)
    return factor_z * (1.0 / jnp.sqrt(frob))


def at_offset(sizes, offset):
    n_gx, n_gy = sizes
    return (
        lax.rem(lax.axis_index("gx") + (offset[0] + n_gx), n_gx),
        lax.rem(lax.axis_index("gy") + (offset[1] + n_gy), n_gy),
    )


def remote(sizes, src, dst, send, recv, offset):
    return pltpu.make_async_remote_copy(
        src_ref=src, dst_ref=dst, send_sem=send, recv_sem=recv,
        device_id=at_offset(sizes, offset), device_id_type=pl.DeviceIdType.MESH,
    )


def greet(sizes, offsets):
    barrier = pltpu.get_barrier_semaphore()
    offsets = sorted({(dx % sizes[0], dy % sizes[1]) for dx, dy in offsets})
    for offset in offsets:
        pl.semaphore_signal(
            barrier, inc=1, device_id=at_offset(sizes, offset),
            device_id_type=pl.DeviceIdType.MESH,
        )
    return lambda: pl.semaphore_wait(barrier, len(offsets))


HALO_OFFSETS = [(dx, dy) for dx, dy, _, _, _ in MESSAGES]


def filter_phase(sizes, inputs, scratch, ready):
    (nodes_in, masses_in, cells_in, down_in, along_in) = inputs
    (nodes, masses, cells, down, along, padded, mass_pad, rim_matrix, inner_matrix, states,
     rim_rounded, inner_rounded, sums, sent_x, sent_y, sent_corner, got_x, got_y, got_corner,
     load_sems, send_sems, recv_sems) = scratch

    loads = [
        pltpu.make_async_copy(src, dst, load_sems.at[index])
        for index, (src, dst) in enumerate(
            [(down_in, down), (along_in, along), (cells_in, cells), (nodes_in, nodes),
             (masses_in, masses)]
        )
    ]
    for load in loads:
        load.start()
    loads[0].wait()
    loads[1].wait()

    rim, inner = slice(0, RIM), slice(RIM, ROWS)
    places = lax.broadcasted_iota(jnp.int32, (216, ROWS), 0)
    to_columns = [one_hot(places == along[c : c + 1, :]).astype(BF16) for c in range(2)]

    def arrange(rows):
        lanes = lax.broadcasted_iota(jnp.int32, (rows.stop - rows.start, 216), 1)
        parts = []
        for c in range(2):
            to_rows = one_hot(lanes == down[rows, c : c + 1]).astype(BF16)
            parts.append(dot(dot(to_rows, cells[0, 0, c]).astype(BF16), to_columns[c]))
        matrix = (parts[0] + parts[1]).astype(BF16)
        rim_matrix[rows] = matrix[:, :RIM]
        inner_matrix[rows] = matrix[:, RIM:]

    loads[2].wait()
    arrange(rim)

    loads[3].wait()

    def load_states(half):
        for x in range(6):
            for z in range(11):
                padded[half, 8 * (11 * x + z) : 8 * (11 * x + z) + 6] = nodes[
                    x, z, :, 128 * half : 128 * half + 128
                ].astype(F32)
        for (x, y), start in STARTS.items():
            for low, skip in ((0, 0), (6, 40)):
                states[0, half, start + low : start + low + 6] = padded[
                    half, pl.ds(88 * x + skip + y, 6, stride=8)
                ]
        rim_rounded[half] = states[0, half, rim].astype(BF16)
        inner_rounded[half] = states[0, half, inner].astype(BF16)

    def load_masses():
        mass_pad[...] = jnp.zeros(mass_pad.shape, F32)
        for x in range(6):
            high, rest = split(masses[x])
            low, least = split(masses[x] - high.astype(F32))
            mass_pad[8 * x : 8 * x + 6, 0:11] = high.astype(F32)
            mass_pad[8 * x : 8 * x + 6, 16:27] = low.astype(F32)
            mass_pad[8 * x : 8 * x + 6, 32:43] = least.astype(F32)
        pick = one_hot(lax.broadcasted_iota(jnp.int32, (ROWS, 48), 1) == down[:, 2:3]).astype(BF16)
        spread = dot(pick, mass_pad[...].astype(BF16))
        lane = lax.broadcasted_iota(jnp.int32, (ROWS, 128), 1)
        return jnp.sum(
            jnp.where(lane % 16 == down[:, 3:4], spread, 0.0), axis=1, keepdims=True
        )

    buffers = {"x": (sent_x, got_x), "y": (sent_y, got_y), "corner": (sent_corner, got_corner)}

    def moves_of(step, half):
        return [
            remote(
                sizes, buffers[kind][0].at[step, half, here], buffers[kind][1].at[step, half, there],
                send_sems.at[step, half, index], recv_sems.at[step, half, index], (dx, dy),
            )
            for index, (dx, dy, kind, here, there) in enumerate(MESSAGES)
        ]

    def advance(step, half, product, rows):
        if step == 0:
            return product * scale1[rows] - shift * states[0, half, rows]
        return (
            (2.0 * product) * scale1[rows]
            - (2.0 * shift) * states[step, half, rows]
            - states[step - 1, half, rows]
        )

    moves = {}

    def launch(step, half, ahead):
        product = ahead + dot(rim_matrix[rim], rim_rounded[half])
        sums[step, half] = product
        corners = [product[12 * i : 12 * i + 12] for i in range(4)]
        for i in range(4):
            sent_corner[step, half, i] = corners[i]
        sent_x[step, half, 0] = jnp.concatenate([corners[0], corners[2], product[48:96]], axis=0)
        sent_x[step, half, 1] = jnp.concatenate([corners[1], corners[3], product[96:144]], axis=0)
        sent_y[step, half, 0] = jnp.concatenate([product[0:24], product[144:192]], axis=0)
        sent_y[step, half, 1] = jnp.concatenate([product[24:48], product[192:240]], axis=0)
        if step == 0 and half == 0:
            ready()
        moves[step, half] = moves_of(step, half)
        for index, move in enumerate(moves[step, half]):
            if step < FILTER_DEG - 1 or index in FIRST:
                move.start()

    def inside(step, half):
        inner_next = advance(
            step,
            half,
            dot(rim_matrix[inner], rim_rounded[half])
            + dot(inner_matrix[inner], inner_rounded[half]),
            inner,
        )
        states[step + 1, half, inner] = inner_next
        if step == FILTER_DEG - 1:
            return inner_next
        inner_rounded[half] = inner_next.astype(BF16)
        return dot(inner_matrix[rim], inner_rounded[half])

    def finish(step, half):
        for move in moves[step, half]:
            move.wait_recv()
        own = sums[step, half]
        x0, x5 = got_x[step, half, 0], got_x[step, half, 1]
        y0, y5 = got_y[step, half, 0], got_y[step, half, 1]
        far = [got_corner[step, half, i] for i in range(4)]
        theirs = jnp.concatenate(
            [
                x0[0:12] + y0[0:12] + far[0],
                x5[0:12] + y0[12:24] + far[1],
                x0[12:24] + y5[0:12] + far[2],
                x5[12:24] + y5[12:24] + far[3],
                x0[24:72],
                x5[24:72],
                y0[24:72],
                y5[24:72],
            ],
            axis=0,
        )
        rim_next = advance(step, half, own + theirs, rim)
        states[step + 1, half, rim] = rim_next
        rim_rounded[half] = rim_next.astype(BF16)
        return rim_next

    for half in range(2):
        load_states(half)
        launch(0, half, dot(inner_matrix[rim], inner_rounded[half]))
    arrange(inner)
    loads[4].wait()
    mass = load_masses()
    weight = mass * down[:, 4:5].astype(F32)
    scale1 = 1.0 / (HALF_SPAN * mass)
    shift = CENTER_SHIFT / HALF_SPAN
    ahead = [inside(0, half) for half in range(2)]
    for step in range(FILTER_DEG - 1):
        for half in range(2):
            finish(step, half)
            launch(step + 1, half, ahead[half])
            ahead[half] = inside(step + 1, half)
    grams = gram(jnp.concatenate(ahead, axis=1), weight[inner])
    last = FILTER_DEG - 1

    def set_last(half, groups, theirs):
        values = []
        for rows, their in zip(groups, theirs):
            values.append(advance(last, half, sums[last, half, rows] + their, rows))
            states[last + 1, half, rows] = values[-1]
        return jnp.concatenate(values, axis=0)

    def finish_owned(half):
        for index in FIRST:
            moves[last, half][index].wait_recv()
        x0, y0 = got_x[last, half, 0], got_y[last, half, 0]
        corner = x0[0:12] + y0[0:12] + got_corner[last, half, 0]
        return set_last(half, OWNED, (corner, x0[24:72], y0[24:72]))

    def start_others(indices):
        for half in range(2):
            for index in indices:
                moves[last, half][index].start()

    def finish_others():
        for half in range(2):
            for index, move in enumerate(moves[last, half]):
                if index not in FIRST:
                    move.wait_recv()
            x0, x5 = got_x[last, half, 0], got_x[last, half, 1]
            y0, y5 = got_y[last, half, 0], got_y[last, half, 1]
            corners = jnp.concatenate(
                [
                    x5[0:12] + y0[12:24] + got_corner[last, half, 1],
                    x0[12:24] + y5[0:12] + got_corner[last, half, 2],
                    x5[12:24] + y5[12:24] + got_corner[last, half, 3],
                ],
                axis=0,
            )
            set_last(half, OTHERS, (corners, x5[24:72], y5[24:72]))

    rims = [finish_owned(half) for half in range(2)]
    rim_weight = jnp.concatenate([weight[rows] for rows in OWNED], axis=0)
    rim_grams = gram(jnp.concatenate(rims, axis=1), rim_weight)
    grams = tuple(a + b for a, b in zip(grams, rim_grams))
    return grams, sum(moves.values(), []), start_others, finish_others


def spread_rows(states, padded, spread):
    padded[...] = jnp.zeros(padded.shape, F32)
    for (x, y), start in STARTS.items():
        for half in range(2):
            padded[half, pl.ds(88 * x + y, 6, stride=8)] = states[half, start : start + 6]
            padded[half, pl.ds(88 * x + 48 + y, 5, stride=8)] = states[
                half, start + 7 : start + 12
            ]
    for half in range(2):
        lanes = slice(128 * half, 128 * half + 128)
        high, low = split(padded[half])
        spread[0, :, lanes] = high
        spread[1, :, lanes] = low


def rotate_phase(spread, factor, out):
    factor_high, factor_low = split(factor)
    result = dot(spread[0], factor_high) + (
        dot(spread[0], factor_low) + dot(spread[1], factor_high)
    )
    for x in range(6):
        for z in range(11):
            low = 8 * (11 * x + z)
            out[x, z] = result[low : low + 6].astype(BF16)


def fused_kernel(sizes, node_total, *refs):
    inputs, out, scratch, extra = refs[:5], refs[5], refs[6:28], refs[28:]
    (spread, own, row_in, part, column_in, whole,
     row_send, row_recv, col_send, col_recv, all_send, all_recv) = extra
    n_gx, n_gy = sizes
    my_y = lax.axis_index("gy")
    ready = greet(
        sizes,
        HALO_OFFSETS + [(0, d) for d in range(1, n_gy)] + [(d, 0) for d in range(1, n_gx)],
    )
    grams, moves, start_others, finish_others = filter_phase(sizes, inputs, scratch, ready)
    pieces, height = own.shape[0], own.shape[2] - 1
    packed, diagonal = pack(grams)
    row_moves, col_moves, all_moves = [], [], []
    for p in range(pieces):
        for index in range(n_gy):
            low = (index * pieces + p) * height
            own[p, index, 0:height] = packed[low : low + height]
            own[p, index, height : height + 1] = diagonal
        row_moves.append([
            remote(sizes, own.at[p, lax.rem(my_y + d, n_gy)], row_in.at[p, d - 1],
                   row_send.at[p, d - 1], row_recv.at[p, d - 1], (0, d))
            for d in range(1, n_gy)
        ])
        for move in row_moves[p]:
            move.start()
        if p == pieces - 1:
            start_others((0, 1, 2, 4))
        col_moves.append([
            remote(sizes, part.at[p], column_in.at[p, d - 1],
                   col_send.at[p, d - 1], col_recv.at[p, d - 1], (d, 0))
            for d in range(1, n_gx)
        ])
        all_moves.append([
            remote(sizes, whole.at[p, my_y], whole.at[p, my_y],
                   all_send.at[p, d - 1], all_recv.at[p, d - 1], (0, d))
            for d in range(1, n_gy)
        ])

    def second(p):
        for move in row_moves[p]:
            move.wait_recv()
        total = own[p, my_y]
        for d in range(1, n_gy):
            total = total + row_in[p, d - 1]
        part[p] = total
        for move in col_moves[p]:
            move.start()

    def third(p):
        for move in col_moves[p]:
            move.wait_recv()
        total = part[p]
        for d in range(1, n_gx):
            total = total + column_in[p, d - 1]
        whole[p, my_y] = total
        for move in all_moves[p]:
            move.start()

    for p in range(pieces):
        second(p)
        if p >= 1:
            third(p - 1)
    start_others((6,))
    third(pieces - 1)
    finish_others()
    spread_rows(scratch[9].at[FILTER_DEG], scratch[5], spread)
    for p in range(pieces):
        for move in all_moves[p]:
            move.wait_recv()
    packed = jnp.concatenate(
        [whole[p, index, 0:height] for index in range(n_gy) for p in range(pieces)], axis=0
    )
    factor = inverse_root(unpack(packed, whole[0, 0, height : height + 1]), node_total)
    rotate_phase(spread, factor, out)
    for move in moves + sum(row_moves + col_moves + all_moves, []):
        move.wait_send()


def filter_kernel(sizes, *refs):
    inputs, filtered, stacked, scratch = refs[:5], refs[5], refs[6], refs[7:]
    grams, moves, start_others, finish_others = filter_phase(
        sizes, inputs, scratch, greet(sizes, HALO_OFFSETS)
    )
    start_others((0, 1, 2, 4, 6))
    finish_others()
    stacked[...] = jnp.concatenate(grams, axis=0)
    filtered[...] = scratch[9][FILTER_DEG]
    for move in moves:
        move.wait_send()


def rotate_kernel(node_total, filtered, stacked, out, padded, spread):
    spread_rows(filtered, padded, spread)
    total = whole_gram(stacked[0:128], stacked[128:256], stacked[256:384])
    rotate_phase(spread, inverse_root(total, node_total), out)


def body(orbitals, masses, cell_matrices):
    n_gx, n_gy = lax.axis_size("gx"), lax.axis_size("gy")
    sizes = (n_gx, n_gy)
    assert orbitals.shape == (6, 6, 11, 256) and cell_matrices.shape == (1, 1, 2, 216, 216)
    node_total = 5 * n_gx * 5 * n_gy * 11
    nodes = jnp.transpose(orbitals, (0, 2, 1, 3))
    down, along = tables()
    arguments = (nodes, masses, cell_matrices, jnp.asarray(down), jnp.asarray(along))
    arguments = tuple(pltpu.with_memory_space_constraint(a, pltpu.HBM) for a in arguments)
    vmem = pl.BlockSpec(memory_space=pltpu.VMEM)
    hbm = pl.BlockSpec(memory_space=pltpu.MemorySpace.HBM)
    filter_scratch = [
        pltpu.VMEM(nodes.shape, BF16),
        pltpu.VMEM(masses.shape, F32),
        pltpu.VMEM(cell_matrices.shape, BF16),
        pltpu.VMEM(down.shape, jnp.int32),
        pltpu.VMEM(along.shape, jnp.int32),
        pltpu.VMEM((2, 528, 128), F32),
        pltpu.VMEM((48, 128), F32),
        pltpu.VMEM((ROWS, RIM), BF16),
        pltpu.VMEM((ROWS, INNER), BF16),
        pltpu.VMEM((FILTER_DEG + 1, 2, ROWS, 128), F32),
        pltpu.VMEM((2, RIM, 128), BF16),
        pltpu.VMEM((2, INNER, 128), BF16),
        pltpu.VMEM((FILTER_DEG, 2, RIM, 128), F32),
    ]
    filter_scratch += [
        pltpu.VMEM((FILTER_DEG, 2) + shape + (128,), F32)
        for shape in ((2, 72), (2, 72), (4, 12)) * 2
    ]
    filter_scratch += [
        pltpu.SemaphoreType.DMA((5,)),
        pltpu.SemaphoreType.DMA((FILTER_DEG, 2, len(MESSAGES))),
        pltpu.SemaphoreType.DMA((FILTER_DEG, 2, len(MESSAGES))),
    ]
    params = pltpu.CompilerParams(
        collective_id=0, has_side_effects=True, vmem_limit_bytes=VMEM_BYTES
    )
    if 256 % (8 * PIECES * n_gy) == 0:
        height = 256 // n_gy // PIECES + 1
        result = pl.pallas_call(
            functools.partial(fused_kernel, sizes, node_total),
            out_shape=pltpu.VMEM(nodes.shape, BF16),
            in_specs=[hbm] * 5,
            out_specs=vmem,
            scratch_shapes=filter_scratch
            + [
                pltpu.VMEM((2, 528, 256), BF16),
                pltpu.VMEM((PIECES, n_gy, height, 128), F32),
                pltpu.VMEM((PIECES, n_gy - 1, height, 128), F32),
                pltpu.VMEM((PIECES, height, 128), F32),
                pltpu.VMEM((PIECES, n_gx - 1, height, 128), F32),
                pltpu.VMEM((PIECES, n_gy, height, 128), F32),
            ]
            + [pltpu.SemaphoreType.DMA((PIECES, n - 1)) for n in (n_gy, n_gy, n_gx, n_gx, n_gy, n_gy)],
            compiler_params=params,
        )(*arguments)
    else:
        filtered, stacked = pl.pallas_call(
            functools.partial(filter_kernel, sizes),
            out_shape=[
                jax.ShapeDtypeStruct((2, ROWS, 128), F32),
                jax.ShapeDtypeStruct((384, 128), F32),
            ],
            in_specs=[hbm] * 5,
            out_specs=[vmem] * 2,
            scratch_shapes=filter_scratch,
            compiler_params=params,
        )(*arguments)
        stacked = lax.psum(stacked, ("gx", "gy"))
        result = pl.pallas_call(
            functools.partial(rotate_kernel, node_total),
            out_shape=jax.ShapeDtypeStruct(nodes.shape, BF16),
            in_specs=[vmem] * 2,
            out_specs=vmem,
            scratch_shapes=[pltpu.VMEM((2, 528, 128), F32), pltpu.VMEM((2, 528, 256), BF16)],
            compiler_params=pltpu.CompilerParams(vmem_limit_bytes=VMEM_BYTES),
        )(filtered, stacked)
    return jnp.transpose(result, (0, 2, 1, 3))


def solution(mesh):
    return jax.shard_map(
        body,
        mesh=mesh,
        in_specs=(P("gx", "gy", None, None), P("gx", "gy", None), P("gx", "gy", None, None, None)),
        out_specs=P("gx", "gy", None, None),
        check_vma=False,
    )
```

```python
import functools

import jax
import jax.numpy as jnp
import numpy as np
from jax import lax
from jax.experimental import pallas as pl
from jax.experimental.pallas import tpu as pltpu
from jax.sharding import PartitionSpec as P

FILTER_DEG = 3
CENTER_SHIFT = 12.0
HALF_SPAN = 12.0

RIM = 240
ROWS = 432
INNER = ROWS - RIM
PIECES = 1
VMEM_BYTES = 24 << 20
BF16 = jnp.bfloat16
F32 = jnp.float32

MESSAGES = (
    (-1, -1, "corner", 0, 3),
    (1, -1, "corner", 1, 2),
    (-1, 1, "corner", 2, 1),
    (1, 1, "corner", 3, 0),
    (-1, 0, "x", 0, 1),
    (1, 0, "x", 1, 0),
    (0, -1, "y", 0, 1),
    (0, 1, "y", 1, 0),
)


PAIRS = (0, 24)
X_FACES, Y_FACES = (48, 96), (144, 192)
GROUPS = tuple((start, 2) for start in PAIRS) + tuple((start, 4) for start in X_FACES + Y_FACES)
GROUPS += ((RIM, 16),)


def column_rows():
    rows = {}

    def add(columns, start):
        for i, column in enumerate(columns):
            rows[column] = (start + 11 * i, start + 11 * len(columns) + i)

    for face in range(2):
        add([(0, 5 * face), (5, 5 * face)], PAIRS[face])
        add([(5 * face, i + 1) for i in range(4)], X_FACES[face])
        add([(i + 1, 5 * face) for i in range(4)], Y_FACES[face])
    add([(i + 1, j + 1) for i in range(4) for j in range(4)], RIM)
    return rows


COLUMNS = column_rows()
FIRST = (3, 5, 7)
ORDER = tuple(("corner", i, j) for j in range(2) for i in range(2))
ORDER += tuple(("x", i, 0) for i in range(2)) + tuple(("y", 0, j) for j in range(2))
OWNED = (slice(0, 11), slice(48, 92), slice(144, 188))
OTHERS = (slice(11, 22), slice(24, 46), slice(96, 140), slice(192, 236))


def tables():
    down = np.zeros((ROWS, 128), np.int32)
    along = np.full((8, ROWS), -1, np.int32)
    for (x, y), (start, double) in COLUMNS.items():
        for z, row in [(z, start + z) for z in range(11)] + [(5, double)]:
            for cell in range(2):
                inside = 0 <= z - 5 * cell <= 5
                down[row, cell] = (x * 6 + y) * 6 + z - 5 * cell if inside else -1
            down[row, 2], down[row, 3] = 8 * x + y, z
            down[row, 4] = int(x < 5 and y < 5 and row != double)
            half = int(z > 5 or row == double)
            along[half, row] = (x * 6 + y) * 6 + z - 5 * half
    return down, along


def dot(a, b):
    return jnp.dot(a, b, preferred_element_type=F32)


def dot_rows(a, b):
    return lax.dot_general(a, b, (((0,), (0,)), ((), ())), preferred_element_type=F32)


def split(a):
    high = a.astype(BF16)
    return high, (a - high.astype(F32)).astype(BF16)


def dot3(a, b):
    a_high, a_low = split(a)
    b_high, b_low = split(b)
    return dot(a_high, b_high) + (dot(a_high, b_low) + dot(a_low, b_high))


def one_hot(condition):
    return jnp.where(condition, 1.0, 0.0).astype(F32)


def gram(rows, weight):
    a_high, a_low = split(rows * weight)
    b_high, b_low = split(rows)

    def part(lanes, columns):
        return dot_rows(a_high[:, lanes], b_high[:, columns]) + (
            dot_rows(a_high[:, lanes], b_low[:, columns])
            + dot_rows(a_low[:, lanes], b_high[:, columns])
        )

    top = part(slice(0, 128), slice(0, 256))
    return top[:, :128], top[:, 128:], part(slice(128, 256), slice(128, 256))


def block_ids():
    return (
        lax.broadcasted_iota(jnp.int32, (128, 128), 0),
        lax.broadcasted_iota(jnp.int32, (128, 128), 1),
    )


def pack(grams):
    s00, s01, s11 = grams
    row, col = block_ids()
    diagonal = jnp.sum(jnp.where(row == col, s11, 0.0), axis=0, keepdims=True)
    return jnp.concatenate([s01, jnp.where(row <= col, s00, s11)], axis=0), diagonal


def unpack(packed, diagonal):
    s01, both = packed[0:128], packed[128:256]
    turned = both.T
    row, col = block_ids()
    s00 = jnp.where(row <= col, both, turned)
    s11 = jnp.where(row > col, both, jnp.where(row < col, turned, diagonal))
    return whole_gram(s00, s01, s11)


def whole_gram(s00, s01, s11):
    top = jnp.concatenate([s00, s01], axis=1)
    bottom = jnp.concatenate([s01.T, s11], axis=1)
    return jnp.concatenate([top, bottom], axis=0)


def inverse_root(gram_sum, node_total):
    inter = gram_sum * (1.0 / node_total)
    inter2 = dot3(inter, inter)
    frob2 = jnp.sum(jnp.sum(inter * inter, axis=0, keepdims=True), axis=1, keepdims=True)
    frob = jnp.sqrt(frob2)
    over = 1.0 / frob
    current = inter * over
    square = (inter2 * over) * over
    row_id = lax.broadcasted_iota(jnp.int32, (256, 256), 0)
    col_id = lax.broadcasted_iota(jnp.int32, (256, 256), 1)
    identity = one_hot(row_id == col_id)
    tail = 0.0625 * square - 0.5625 * current
    factor_z = 2.25 * identity - 2.4375 * current + 1.6875 * square
    factor_z = factor_z + dot(square.astype(BF16), tail.astype(BF16))
    return factor_z * (1.0 / jnp.sqrt(frob))


def at_offset(sizes, offset):
    n_gx, n_gy = sizes
    return (
        lax.rem(lax.axis_index("gx") + (offset[0] + n_gx), n_gx),
        lax.rem(lax.axis_index("gy") + (offset[1] + n_gy), n_gy),
    )


def remote(sizes, src, dst, send, recv, offset):
    return pltpu.make_async_remote_copy(
        src_ref=src, dst_ref=dst, send_sem=send, recv_sem=recv,
        device_id=at_offset(sizes, offset), device_id_type=pl.DeviceIdType.MESH,
    )


def greet(sizes, offsets):
    barrier = pltpu.get_barrier_semaphore()
    offsets = sorted({(dx % sizes[0], dy % sizes[1]) for dx, dy in offsets})
    for offset in offsets:
        pl.semaphore_signal(
            barrier, inc=1, device_id=at_offset(sizes, offset),
            device_id_type=pl.DeviceIdType.MESH,
        )
    return lambda: pl.semaphore_wait(barrier, len(offsets))


HALO_OFFSETS = [(dx, dy) for dx, dy, _, _, _ in MESSAGES]


def filter_phase(sizes, inputs, scratch, ready):
    (nodes_in, masses_in, cells_in, down_in, along_in) = inputs
    (nodes, masses, cells, down, along, padded, mass_pad, rim_matrix, inner_matrix, states,
     rim_rounded, inner_rounded, sums, sent_x, sent_y, sent_corner, got_x, got_y, got_corner,
     load_sems, send_sems, recv_sems) = scratch
    last = FILTER_DEG - 1

    loads = [
        pltpu.make_async_copy(src, dst, load_sems.at[index])
        for index, (src, dst) in enumerate(
            [(down_in, down), (along_in, along), (cells_in, cells), (nodes_in, nodes),
             (masses_in, masses)]
        )
    ]
    for load in loads:
        load.start()
    loads[0].wait()
    loads[1].wait()

    rim, inner = slice(0, RIM), slice(RIM, ROWS)
    places = lax.broadcasted_iota(jnp.int32, (216, ROWS), 0)
    to_columns = [one_hot(places == along[c : c + 1, :]).astype(BF16) for c in range(2)]

    def arrange(rows):
        lanes = lax.broadcasted_iota(jnp.int32, (rows.stop - rows.start, 216), 1)
        parts = []
        for c in range(2):
            to_rows = one_hot(lanes == down[rows, c : c + 1]).astype(BF16)
            parts.append(dot(dot(to_rows, cells[0, 0, c]).astype(BF16), to_columns[c]))
        matrix = (parts[0] + parts[1]).astype(BF16)
        rim_matrix[rows] = matrix[:, :RIM]
        inner_matrix[rows] = matrix[:, RIM:]

    loads[2].wait()
    arrange(rim)

    loads[3].wait()

    def load_states(half):
        for x in range(6):
            for z in range(11):
                padded[half, 8 * (11 * x + z) : 8 * (11 * x + z) + 6] = nodes[
                    x, z, :, 128 * half : 128 * half + 128
                ].astype(F32)
        for (x, y), (start, _) in COLUMNS.items():
            states[0, half, start : start + 11] = padded[half, pl.ds(88 * x + y, 11, stride=8)]
        for start, count in GROUPS:
            states[0, half, start + 11 * count : start + 12 * count] = states[
                0, half, pl.ds(start + 5, count, stride=11)
            ]
        rim_rounded[half] = states[0, half, rim].astype(BF16)
        inner_rounded[half] = states[0, half, inner].astype(BF16)

    def load_masses():
        mass_pad[...] = jnp.zeros(mass_pad.shape, F32)
        for x in range(6):
            high, rest = split(masses[x])
            low, least = split(masses[x] - high.astype(F32))
            mass_pad[8 * x : 8 * x + 6, 0:11] = high.astype(F32)
            mass_pad[8 * x : 8 * x + 6, 16:27] = low.astype(F32)
            mass_pad[8 * x : 8 * x + 6, 32:43] = least.astype(F32)
        pick = one_hot(lax.broadcasted_iota(jnp.int32, (ROWS, 48), 1) == down[:, 2:3]).astype(BF16)
        spread = dot(pick, mass_pad[...].astype(BF16))
        lane = lax.broadcasted_iota(jnp.int32, (ROWS, 128), 1)
        return jnp.sum(
            jnp.where(lane % 16 == down[:, 3:4], spread, 0.0), axis=1, keepdims=True
        )

    side = lax.rem(lax.axis_index("gy"), 2)

    def pick(here, there):
        return jnp.where(side == 0, here, there)

    buffers = {"x": (sent_x, got_x), "y": (sent_y, got_y), "corner": (sent_corner, got_corner)}

    def moves_of(step, half):
        return [
            remote(
                sizes, buffers[kind][0].at[step, half, here], buffers[kind][1].at[step, half, there],
                send_sems.at[step, half, index], recv_sems.at[step, half, index], (dx, dy),
            )
            for index, (dx, dy, kind, here, there) in enumerate(MESSAGES)
        ]

    def advance(step, half, product, rows):
        if step == 0:
            return product * scale1[rows] - shift * states[0, half, rows]
        return (
            (2.0 * product) * scale1[rows]
            - (2.0 * shift) * states[step, half, rows]
            - states[step - 1, half, rows]
        )

    turn = lax.rem(lax.axis_index("gy"), 2)

    def ordered_moves(step, half):
        moves = []
        for kind, i, j in ORDER:
            f, g = turn + i * (1 - 2 * turn), turn + j * (1 - 2 * turn)
            here, slot, count, offset = {
                "corner": (f + 2 * g, f + 2 * g, 4, (2 * f - 1, 2 * g - 1)),
                "x": (f, 4 + f, 2, (2 * f - 1, 0)),
                "y": (g, 6 + g, 2, (0, 2 * g - 1)),
            }[kind]
            moves.append(
                remote(
                    sizes, buffers[kind][0].at[step, half, here],
                    buffers[kind][1].at[step, half, count - 1 - here],
                    send_sems.at[step, half, slot], recv_sems.at[step, half, slot], offset,
                )
            )
        return moves

    moves = {}

    def launch(step, half, ahead):
        moves[step, half] = moves_of(step, half)
        order = [moves[step, half][i] for i in FIRST] if step == last else ordered_moves(step, half)
        first = 1 if step == last else 4
        pair_rows, face_rows = slice(0, X_FACES[0]), slice(X_FACES[0], RIM)
        product = ahead[pair_rows] + dot(rim_matrix[pair_rows], rim_rounded[half])
        sums[step, half, pair_rows] = product
        pairs = [product[start : start + 22] for start in PAIRS]
        for g in range(2):
            for f in range(2):
                sent_corner[step, half, f + 2 * g] = pairs[g][11 * f : 11 * f + 11]
        if step == 0 and half == 0:
            ready()
        for move in order[:first]:
            move.start()
        product = ahead[face_rows] + dot(rim_matrix[face_rows], rim_rounded[half])
        sums[step, half, face_rows] = product
        for f in range(2):
            low = slice(11 * f, 11 * f + 11)
            x_face = product[X_FACES[f] - X_FACES[0] :][:44]
            y_face = product[Y_FACES[f] - X_FACES[0] :][:44]
            sent_x[step, half, f] = jnp.concatenate([x_face, pairs[0][low], pairs[1][low]], axis=0)
            sent_y[step, half, f] = jnp.concatenate([y_face, pairs[f]], axis=0)
        for move in order[first:]:
            move.start()

    def inside(step, half):
        inner_next = advance(
            step,
            half,
            dot(rim_matrix[inner], rim_rounded[half])
            + dot(inner_matrix[inner], inner_rounded[half]),
            inner,
        )
        states[step + 1, half, inner] = inner_next
        if step == FILTER_DEG - 1:
            return inner_next
        inner_rounded[half] = inner_next.astype(BF16)
        return dot(inner_matrix[rim], inner_rounded[half])

    def finish(step, half):
        for move in moves[step, half]:
            move.wait_recv()
        theirs = []
        for g in range(2):
            low = slice(44 + 11 * g, 55 + 11 * g)
            pair = got_y[step, half, g, 44:66] + jnp.concatenate(
                [got_x[step, half, f, low] + got_corner[step, half, f + 2 * g] for f in range(2)],
                axis=0,
            )
            theirs += [pair, pair[5:6], pair[16:17]]
        for got in (got_x, got_y):
            for f in range(2):
                theirs += [
                    got[step, half, f, 0:44],
                    got[step, half, f, pl.ds(5, 4, stride=11)],
                ]
        rim_next = advance(
            step, half, sums[step, half] + jnp.concatenate(theirs, axis=0), rim
        )
        states[step + 1, half, rim] = rim_next
        rim_rounded[half] = rim_next.astype(BF16)

    for half in range(2):
        load_states(half)
        launch(0, half, dot(inner_matrix[rim], inner_rounded[half]))
    arrange(inner)
    loads[4].wait()
    mass = load_masses()
    weight = mass * down[:, 4:5].astype(F32)
    scale1 = 1.0 / (HALF_SPAN * mass)
    shift = CENTER_SHIFT / HALF_SPAN
    ahead = [inside(0, half) for half in range(2)]
    for step in range(last):
        for half in range(2):
            finish(step, half)
            launch(step + 1, half, ahead[half])
            ahead[half] = inside(step + 1, half)
    grams = gram(jnp.concatenate(ahead, axis=1), weight[inner])

    def set_last(half, groups, theirs):
        values = []
        for rows, their in zip(groups, theirs):
            values.append(advance(last, half, sums[last, half, rows] + their, rows))
            states[last + 1, half, rows] = values[-1]
        return jnp.concatenate(values, axis=0)

    def finish_owned(half):
        for index in FIRST:
            moves[last, half][index].wait_recv()
        x0, y0 = got_x[last, half, 0], got_y[last, half, 0]
        corner = x0[44:55] + y0[44:55] + got_corner[last, half, 0]
        return set_last(half, OWNED, (corner, x0[0:44], y0[0:44]))

    def start_others(indices):
        for half in range(2):
            for index in indices:
                moves[last, half][index].start()

    def finish_others():
        for half in range(2):
            for index, move in enumerate(moves[last, half]):
                if index not in FIRST:
                    move.wait_recv()
            x0, x5 = got_x[last, half, 0], got_x[last, half, 1]
            y0, y5 = got_y[last, half, 0], got_y[last, half, 1]
            corners = [got_corner[last, half, i] for i in range(4)]
            pair = jnp.concatenate(
                [x0[55:66] + y5[44:55] + corners[2], x5[55:66] + y5[55:66] + corners[3]], axis=0
            )
            corner = x5[44:55] + y0[55:66] + corners[1]
            set_last(half, OTHERS, (corner, pair, x5[0:44], y5[0:44]))

    rims = [finish_owned(half) for half in range(2)]
    rim_weight = jnp.concatenate([weight[rows] for rows in OWNED], axis=0)
    rim_grams = gram(jnp.concatenate(rims, axis=1), rim_weight)
    grams = tuple(a + b for a, b in zip(grams, rim_grams))
    return grams, sum(moves.values(), []), start_others, finish_others


def spread_rows(states, padded, spread):
    padded[...] = jnp.zeros(padded.shape, F32)
    for (x, y), (start, _) in COLUMNS.items():
        for half in range(2):
            padded[half, pl.ds(88 * x + y, 11, stride=8)] = states[half, start : start + 11]
    for half in range(2):
        lanes = slice(128 * half, 128 * half + 128)
        high, low = split(padded[half])
        spread[0, :, lanes] = high
        spread[1, :, lanes] = low


def rotate_phase(spread, factor, out):
    factor_high, factor_low = split(factor)
    result = dot(spread[0], factor_high) + (
        dot(spread[0], factor_low) + dot(spread[1], factor_high)
    )
    for x in range(6):
        for z in range(11):
            low = 8 * (11 * x + z)
            out[x, z] = result[low : low + 6].astype(BF16)


def fused_kernel(sizes, node_total, *refs):
    inputs, out, scratch, extra = refs[:5], refs[5], refs[6:28], refs[28:]
    (spread, own, row_in, part, column_in, whole,
     row_send, row_recv, col_send, col_recv, all_send, all_recv) = extra
    n_gx, n_gy = sizes
    my_y = lax.axis_index("gy")
    ready = greet(
        sizes,
        HALO_OFFSETS + [(0, d) for d in range(1, n_gy)] + [(d, 0) for d in range(1, n_gx)],
    )
    grams, moves, start_others, finish_others = filter_phase(sizes, inputs, scratch, ready)
    pieces, height = own.shape[0], own.shape[2] - 1
    packed, diagonal = pack(grams)
    row_moves, col_moves, all_moves = [], [], []
    for p in range(pieces):
        for index in range(n_gy):
            low = (index * pieces + p) * height
            own[p, index, 0:height] = packed[low : low + height]
            own[p, index, height : height + 1] = diagonal
        row_moves.append([
            remote(sizes, own.at[p, lax.rem(my_y + d, n_gy)], row_in.at[p, d - 1],
                   row_send.at[p, d - 1], row_recv.at[p, d - 1], (0, d))
            for d in range(1, n_gy)
        ])
        for move in row_moves[p]:
            move.start()
        if p == pieces - 1:
            start_others((0, 1, 2, 4))
        col_moves.append([
            remote(sizes, part.at[p], column_in.at[p, d - 1],
                   col_send.at[p, d - 1], col_recv.at[p, d - 1], (d, 0))
            for d in range(1, n_gx)
        ])
        all_moves.append([
            remote(sizes, whole.at[p, my_y], whole.at[p, my_y],
                   all_send.at[p, d - 1], all_recv.at[p, d - 1], (0, d))
            for d in range(1, n_gy)
        ])

    def second(p):
        for move in row_moves[p]:
            move.wait_recv()
        total = own[p, my_y]
        for d in range(1, n_gy):
            total = total + row_in[p, d - 1]
        part[p] = total
        for move in col_moves[p]:
            move.start()

    def third(p):
        for move in col_moves[p]:
            move.wait_recv()
        total = part[p]
        for d in range(1, n_gx):
            total = total + column_in[p, d - 1]
        whole[p, my_y] = total
        for move in all_moves[p]:
            move.start()

    for p in range(pieces):
        second(p)
        if p >= 1:
            third(p - 1)
    start_others((6,))
    third(pieces - 1)
    finish_others()
    spread_rows(scratch[9].at[FILTER_DEG], scratch[5], spread)
    for p in range(pieces):
        for move in all_moves[p]:
            move.wait_recv()
    packed = jnp.concatenate(
        [whole[p, index, 0:height] for index in range(n_gy) for p in range(pieces)], axis=0
    )
    factor = inverse_root(unpack(packed, whole[0, 0, height : height + 1]), node_total)
    rotate_phase(spread, factor, out)
    for move in moves + sum(row_moves + col_moves + all_moves, []):
        move.wait_send()


def filter_kernel(sizes, *refs):
    inputs, filtered, stacked, scratch = refs[:5], refs[5], refs[6], refs[7:]
    grams, moves, start_others, finish_others = filter_phase(
        sizes, inputs, scratch, greet(sizes, HALO_OFFSETS)
    )
    start_others((0, 1, 2, 4, 6))
    finish_others()
    stacked[...] = jnp.concatenate(grams, axis=0)
    filtered[...] = scratch[9][FILTER_DEG]
    for move in moves:
        move.wait_send()


def rotate_kernel(node_total, filtered, stacked, out, padded, spread):
    spread_rows(filtered, padded, spread)
    total = whole_gram(stacked[0:128], stacked[128:256], stacked[256:384])
    rotate_phase(spread, inverse_root(total, node_total), out)


def body(orbitals, masses, cell_matrices):
    n_gx, n_gy = lax.axis_size("gx"), lax.axis_size("gy")
    sizes = (n_gx, n_gy)
    assert n_gy % 2 == 0
    assert orbitals.shape == (6, 6, 11, 256) and cell_matrices.shape == (1, 1, 2, 216, 216)
    node_total = 5 * n_gx * 5 * n_gy * 11
    nodes = jnp.transpose(orbitals, (0, 2, 1, 3))
    down, along = tables()
    arguments = (nodes, masses, cell_matrices, jnp.asarray(down), jnp.asarray(along))
    arguments = tuple(pltpu.with_memory_space_constraint(a, pltpu.HBM) for a in arguments)
    vmem = pl.BlockSpec(memory_space=pltpu.VMEM)
    hbm = pl.BlockSpec(memory_space=pltpu.MemorySpace.HBM)
    filter_scratch = [
        pltpu.VMEM(nodes.shape, BF16),
        pltpu.VMEM(masses.shape, F32),
        pltpu.VMEM(cell_matrices.shape, BF16),
        pltpu.VMEM(down.shape, jnp.int32),
        pltpu.VMEM(along.shape, jnp.int32),
        pltpu.VMEM((2, 528, 128), F32),
        pltpu.VMEM((48, 128), F32),
        pltpu.VMEM((ROWS, RIM), BF16),
        pltpu.VMEM((ROWS, INNER), BF16),
        pltpu.VMEM((FILTER_DEG + 1, 2, ROWS, 128), F32),
        pltpu.VMEM((2, RIM, 128), BF16),
        pltpu.VMEM((2, INNER, 128), BF16),
        pltpu.VMEM((FILTER_DEG, 2, RIM, 128), F32),
    ]
    filter_scratch += [
        pltpu.VMEM((FILTER_DEG, 2) + shape + (128,), F32)
        for shape in ((2, 66), (2, 66), (4, 11)) * 2
    ]
    filter_scratch += [
        pltpu.SemaphoreType.DMA((5,)),
        pltpu.SemaphoreType.DMA((FILTER_DEG, 2, len(MESSAGES))),
        pltpu.SemaphoreType.DMA((FILTER_DEG, 2, len(MESSAGES))),
    ]
    params = pltpu.CompilerParams(
        collective_id=0, has_side_effects=True, vmem_limit_bytes=VMEM_BYTES
    )
    if 256 % (8 * PIECES * n_gy) == 0:
        height = 256 // n_gy // PIECES + 1
        result = pl.pallas_call(
            functools.partial(fused_kernel, sizes, node_total),
            out_shape=pltpu.VMEM(nodes.shape, BF16),
            in_specs=[hbm] * 5,
            out_specs=vmem,
            scratch_shapes=filter_scratch
            + [
                pltpu.VMEM((2, 528, 256), BF16),
                pltpu.VMEM((PIECES, n_gy, height, 128), F32),
                pltpu.VMEM((PIECES, n_gy - 1, height, 128), F32),
                pltpu.VMEM((PIECES, height, 128), F32),
                pltpu.VMEM((PIECES, n_gx - 1, height, 128), F32),
                pltpu.VMEM((PIECES, n_gy, height, 128), F32),
            ]
            + [pltpu.SemaphoreType.DMA((PIECES, n - 1)) for n in (n_gy, n_gy, n_gx, n_gx, n_gy, n_gy)],
            compiler_params=params,
        )(*arguments)
    else:
        filtered, stacked = pl.pallas_call(
            functools.partial(filter_kernel, sizes),
            out_shape=[
                jax.ShapeDtypeStruct((2, ROWS, 128), F32),
                jax.ShapeDtypeStruct((384, 128), F32),
            ],
            in_specs=[hbm] * 5,
            out_specs=[vmem] * 2,
            scratch_shapes=filter_scratch,
            compiler_params=params,
        )(*arguments)
        stacked = lax.psum(stacked, ("gx", "gy"))
        result = pl.pallas_call(
            functools.partial(rotate_kernel, node_total),
            out_shape=jax.ShapeDtypeStruct(nodes.shape, BF16),
            in_specs=[vmem] * 2,
            out_specs=vmem,
            scratch_shapes=[pltpu.VMEM((2, 528, 128), F32), pltpu.VMEM((2, 528, 256), BF16)],
            compiler_params=pltpu.CompilerParams(vmem_limit_bytes=VMEM_BYTES),
        )(filtered, stacked)
    return jnp.transpose(result, (0, 2, 1, 3))


def solution(mesh):
    return jax.shard_map(
        body,
        mesh=mesh,
        in_specs=(P("gx", "gy", None, None), P("gx", "gy", None), P("gx", "gy", None, None, None)),
        out_specs=P("gx", "gy", None, None),
        check_vma=False,
    )
```

```python
import functools

import jax
import jax.numpy as jnp
import numpy as np
from jax import lax
from jax.experimental import pallas as pl
from jax.experimental.pallas import tpu as pltpu
from jax.sharding import PartitionSpec as P

FILTER_DEG = 3
CENTER_SHIFT = 12.0
HALF_SPAN = 12.0

RIM = 240
ROWS = 432
INNER = ROWS - RIM
PIECES = 1
VMEM_BYTES = 24 << 20
BF16 = jnp.bfloat16
F32 = jnp.float32

MESSAGES = (
    (-1, -1, "corner", 0, 3),
    (1, -1, "corner", 1, 2),
    (-1, 1, "corner", 2, 1),
    (1, 1, "corner", 3, 0),
    (-1, 0, "x", 0, 1),
    (1, 0, "x", 1, 0),
    (0, -1, "y", 0, 1),
    (0, 1, "y", 1, 0),
)


PAIRS = (0, 24)
X_FACES, Y_FACES = (48, 96), (144, 192)
GROUPS = tuple((start, 2) for start in PAIRS) + tuple((start, 4) for start in X_FACES + Y_FACES)
GROUPS += ((RIM, 16),)


def column_rows():
    rows = {}

    def add(columns, start):
        for i, column in enumerate(columns):
            rows[column] = (start + 11 * i, start + 11 * len(columns) + i)

    for face in range(2):
        add([(0, 5 * face), (5, 5 * face)], PAIRS[face])
        add([(5 * face, i + 1) for i in range(4)], X_FACES[face])
        add([(i + 1, 5 * face) for i in range(4)], Y_FACES[face])
    add([(i + 1, j + 1) for i in range(4) for j in range(4)], RIM)
    return rows


COLUMNS = column_rows()
FIRST = (3, 5, 7)
ORDER = tuple(("corner", i, j) for j in range(2) for i in range(2))
ORDER += tuple(("x", i, 0) for i in range(2)) + tuple(("y", 0, j) for j in range(2))
OWNED = (slice(0, 11), slice(48, 92), slice(144, 188))
OTHERS = (slice(11, 22), slice(24, 46), slice(96, 140), slice(192, 236))


def tables():
    down = np.zeros((ROWS, 128), np.int32)
    along = np.full((8, ROWS), -1, np.int32)
    for (x, y), (start, double) in COLUMNS.items():
        for z, row in [(z, start + z) for z in range(11)] + [(5, double)]:
            for cell in range(2):
                inside = 0 <= z - 5 * cell <= 5
                down[row, cell] = (x * 6 + y) * 6 + z - 5 * cell if inside else -1
            down[row, 2], down[row, 3] = 8 * x + y, z
            down[row, 4] = int(x < 5 and y < 5 and row != double)
            half = int(z > 5 or row == double)
            along[half, row] = (x * 6 + y) * 6 + z - 5 * half
    return down, along


def dot(a, b):
    return jnp.dot(a, b, preferred_element_type=F32)


def dot_rows(a, b):
    return lax.dot_general(a, b, (((0,), (0,)), ((), ())), preferred_element_type=F32)


def split(a):
    high = a.astype(BF16)
    return high, (a - high.astype(F32)).astype(BF16)


def dot3(a, b):
    a_high, a_low = split(a)
    b_high, b_low = split(b)
    return dot(a_high, b_high) + (dot(a_high, b_low) + dot(a_low, b_high))


def one_hot(condition):
    return jnp.where(condition, 1.0, 0.0).astype(F32)


def gram(rows, weight):
    a_high, a_low = split(rows * weight)
    b_high, b_low = split(rows)

    def part(lanes, columns):
        return dot_rows(a_high[:, lanes], b_high[:, columns]) + (
            dot_rows(a_high[:, lanes], b_low[:, columns])
            + dot_rows(a_low[:, lanes], b_high[:, columns])
        )

    top = part(slice(0, 128), slice(0, 256))
    return top[:, :128], top[:, 128:], part(slice(128, 256), slice(128, 256))


def block_ids():
    return (
        lax.broadcasted_iota(jnp.int32, (128, 128), 0),
        lax.broadcasted_iota(jnp.int32, (128, 128), 1),
    )


def pack(grams):
    s00, s01, s11 = grams
    row, col = block_ids()
    diagonal = jnp.sum(jnp.where(row == col, s11, 0.0), axis=0, keepdims=True)
    return jnp.concatenate([s01, jnp.where(row <= col, s00, s11)], axis=0), diagonal


def unpack(packed, diagonal):
    s01, both = packed[0:128], packed[128:256]
    turned = both.T
    row, col = block_ids()
    s00 = jnp.where(row <= col, both, turned)
    s11 = jnp.where(row > col, both, jnp.where(row < col, turned, diagonal))
    return whole_gram(s00, s01, s11)


def whole_gram(s00, s01, s11):
    top = jnp.concatenate([s00, s01], axis=1)
    bottom = jnp.concatenate([s01.T, s11], axis=1)
    return jnp.concatenate([top, bottom], axis=0)


def inverse_root(gram_sum, node_total):
    inter = gram_sum * (1.0 / node_total)
    inter2 = dot3(inter, inter)
    frob2 = jnp.sum(jnp.sum(inter * inter, axis=0, keepdims=True), axis=1, keepdims=True)
    frob = jnp.sqrt(frob2)
    over = 1.0 / frob
    current = inter * over
    square = (inter2 * over) * over
    row_id = lax.broadcasted_iota(jnp.int32, (256, 256), 0)
    col_id = lax.broadcasted_iota(jnp.int32, (256, 256), 1)
    identity = one_hot(row_id == col_id)
    tail = 0.0625 * square - 0.5625 * current
    factor_z = 2.25 * identity - 2.4375 * current + 1.6875 * square
    factor_z = factor_z + dot(square.astype(BF16), tail.astype(BF16))
    return factor_z * (1.0 / jnp.sqrt(frob))


def at_offset(sizes, offset):
    n_gx, n_gy = sizes
    return (
        lax.rem(lax.axis_index("gx") + (offset[0] + n_gx), n_gx),
        lax.rem(lax.axis_index("gy") + (offset[1] + n_gy), n_gy),
    )


def remote(sizes, src, dst, send, recv, offset):
    return pltpu.make_async_remote_copy(
        src_ref=src, dst_ref=dst, send_sem=send, recv_sem=recv,
        device_id=at_offset(sizes, offset), device_id_type=pl.DeviceIdType.MESH,
    )


def greet(sizes, offsets):
    barrier = pltpu.get_barrier_semaphore()
    offsets = sorted({(dx % sizes[0], dy % sizes[1]) for dx, dy in offsets})
    for offset in offsets:
        pl.semaphore_signal(
            barrier, inc=1, device_id=at_offset(sizes, offset),
            device_id_type=pl.DeviceIdType.MESH,
        )
    return lambda: pl.semaphore_wait(barrier, len(offsets))


HALO_OFFSETS = [(dx, dy) for dx, dy, _, _, _ in MESSAGES]


def filter_phase(sizes, inputs, scratch, ready):
    (nodes_in, masses_in, cells_in, down_in, along_in) = inputs
    (nodes, masses, cells, down, along, padded, mass_pad, rim_matrix, inner_matrix, states,
     rim_rounded, inner_rounded, sums, sent_x, sent_y, sent_corner, got_x, got_y, got_corner,
     load_sems, send_sems, recv_sems) = scratch
    last = FILTER_DEG - 1

    loads = [
        pltpu.make_async_copy(src, dst, load_sems.at[index])
        for index, (src, dst) in enumerate(
            [(down_in, down), (along_in, along), (cells_in, cells), (nodes_in, nodes),
             (masses_in, masses)]
        )
    ]
    for load in loads:
        load.start()
    loads[0].wait()
    loads[1].wait()

    rim, inner = slice(0, RIM), slice(RIM, ROWS)
    places = lax.broadcasted_iota(jnp.int32, (216, ROWS), 0)
    to_columns = [one_hot(places == along[c : c + 1, :]).astype(BF16) for c in range(2)]

    def arrange(rows):
        lanes = lax.broadcasted_iota(jnp.int32, (rows.stop - rows.start, 216), 1)
        parts = []
        for c in range(2):
            to_rows = one_hot(lanes == down[rows, c : c + 1]).astype(BF16)
            parts.append(dot(dot(to_rows, cells[0, 0, c]).astype(BF16), to_columns[c]))
        matrix = (parts[0] + parts[1]).astype(BF16)
        rim_matrix[rows] = matrix[:, :RIM]
        inner_matrix[rows] = matrix[:, RIM:]

    loads[2].wait()
    arrange(rim)

    loads[3].wait()

    def load_states(half):
        for x in range(6):
            for z in range(11):
                padded[half, 8 * (11 * x + z) : 8 * (11 * x + z) + 6] = nodes[
                    x, z, :, 128 * half : 128 * half + 128
                ].astype(F32)
        for (x, y), (start, _) in COLUMNS.items():
            states[0, half, start : start + 11] = padded[half, pl.ds(88 * x + y, 11, stride=8)]
        for start, count in GROUPS:
            states[0, half, start + 11 * count : start + 12 * count] = states[
                0, half, pl.ds(start + 5, count, stride=11)
            ]
        rim_rounded[half] = states[0, half, rim].astype(BF16)
        inner_rounded[half] = states[0, half, inner].astype(BF16)

    def load_masses():
        mass_pad[...] = jnp.zeros(mass_pad.shape, F32)
        for x in range(6):
            high, rest = split(masses[x])
            low, least = split(masses[x] - high.astype(F32))
            mass_pad[8 * x : 8 * x + 6, 0:11] = high.astype(F32)
            mass_pad[8 * x : 8 * x + 6, 16:27] = low.astype(F32)
            mass_pad[8 * x : 8 * x + 6, 32:43] = least.astype(F32)
        pick = one_hot(lax.broadcasted_iota(jnp.int32, (ROWS, 48), 1) == down[:, 2:3]).astype(BF16)
        spread = dot(pick, mass_pad[...].astype(BF16))
        lane = lax.broadcasted_iota(jnp.int32, (ROWS, 128), 1)
        return jnp.sum(
            jnp.where(lane % 16 == down[:, 3:4], spread, 0.0), axis=1, keepdims=True
        )

    side = lax.rem(lax.axis_index("gy"), 2)

    def pick(here, there):
        return jnp.where(side == 0, here, there)

    buffers = {"x": (sent_x, got_x), "y": (sent_y, got_y), "corner": (sent_corner, got_corner)}

    def moves_of(step, half):
        return [
            remote(
                sizes, buffers[kind][0].at[step, half, here], buffers[kind][1].at[step, half, there],
                send_sems.at[step, half, index], recv_sems.at[step, half, index], (dx, dy),
            )
            for index, (dx, dy, kind, here, there) in enumerate(MESSAGES)
        ]

    def advance(step, half, product, rows):
        if step == 0:
            return product * scale1[rows] - shift * states[0, half, rows]
        return (
            (2.0 * product) * scale1[rows]
            - (2.0 * shift) * states[step, half, rows]
            - states[step - 1, half, rows]
        )

    turn = lax.rem(lax.axis_index("gy"), 2)

    def ordered_moves(step, half):
        moves = []
        for kind, i, j in ORDER:
            f, g = turn + i * (1 - 2 * turn), turn + j * (1 - 2 * turn)
            here, slot, count, offset = {
                "corner": (f + 2 * g, f + 2 * g, 4, (2 * f - 1, 2 * g - 1)),
                "x": (f, 4 + f, 2, (2 * f - 1, 0)),
                "y": (g, 6 + g, 2, (0, 2 * g - 1)),
            }[kind]
            moves.append(
                remote(
                    sizes, buffers[kind][0].at[step, half, here],
                    buffers[kind][1].at[step, half, count - 1 - here],
                    send_sems.at[step, half, slot], recv_sems.at[step, half, slot], offset,
                )
            )
        return moves

    moves = {}

    def launch(step, half, ahead):
        moves[step, half] = moves_of(step, half)
        order = [moves[step, half][i] for i in FIRST] if step == last else ordered_moves(step, half)
        first = 1 if step == last else 4
        pair_rows, face_rows = slice(0, X_FACES[0]), slice(X_FACES[0], RIM)
        product = ahead[pair_rows] + dot(rim_matrix[pair_rows], rim_rounded[half])
        sums[step, half, pair_rows] = product
        pairs = [product[start : start + 22] for start in PAIRS]
        for g in range(2):
            for f in range(2):
                sent_corner[step, half, f + 2 * g] = pairs[g][11 * f : 11 * f + 11]
        if step == 0 and half == 0:
            ready()
        for move in order[:first]:
            move.start()
        product = ahead[face_rows] + dot(rim_matrix[face_rows], rim_rounded[half])
        sums[step, half, face_rows] = product
        for f in range(2):
            low = slice(11 * f, 11 * f + 11)
            x_face = product[X_FACES[f] - X_FACES[0] :][:44]
            y_face = product[Y_FACES[f] - X_FACES[0] :][:44]
            sent_x[step, half, f] = jnp.concatenate([x_face, pairs[0][low], pairs[1][low]], axis=0)
            sent_y[step, half, f] = jnp.concatenate([y_face, pairs[f]], axis=0)
        for move in order[first:]:
            move.start()

    def inside(step, half):
        inner_next = advance(
            step,
            half,
            dot(rim_matrix[inner], rim_rounded[half])
            + dot(inner_matrix[inner], inner_rounded[half]),
            inner,
        )
        states[step + 1, half, inner] = inner_next
        if step == FILTER_DEG - 1:
            return inner_next
        inner_rounded[half] = inner_next.astype(BF16)
        return dot(inner_matrix[rim], inner_rounded[half])

    def finish(step, half):
        for move in moves[step, half]:
            move.wait_recv()
        theirs = []
        for g in range(2):
            low = slice(44 + 11 * g, 55 + 11 * g)
            pair = got_y[step, half, g, 44:66] + jnp.concatenate(
                [got_x[step, half, f, low] + got_corner[step, half, f + 2 * g] for f in range(2)],
                axis=0,
            )
            theirs += [pair, pair[5:6], pair[16:17]]
        for got in (got_x, got_y):
            for f in range(2):
                theirs += [
                    got[step, half, f, 0:44],
                    got[step, half, f, pl.ds(5, 4, stride=11)],
                ]
        rim_next = advance(
            step, half, sums[step, half] + jnp.concatenate(theirs, axis=0), rim
        )
        states[step + 1, half, rim] = rim_next
        rim_rounded[half] = rim_next.astype(BF16)

    for half in range(2):
        load_states(half)
        launch(0, half, dot(inner_matrix[rim], inner_rounded[half]))
    arrange(inner)
    loads[4].wait()
    mass = load_masses()
    weight = mass * down[:, 4:5].astype(F32)
    scale1 = 1.0 / (HALF_SPAN * mass)
    shift = CENTER_SHIFT / HALF_SPAN
    ahead = [inside(0, half) for half in range(2)]
    for step in range(last):
        for half in range(2):
            finish(step, half)
            launch(step + 1, half, ahead[half])
            ahead[half] = inside(step + 1, half)
    grams = gram(jnp.concatenate(ahead, axis=1), weight[inner])

    def set_last(half, groups, theirs):
        values = []
        for rows, their in zip(groups, theirs):
            values.append(advance(last, half, sums[last, half, rows] + their, rows))
            states[last + 1, half, rows] = values[-1]
        return jnp.concatenate(values, axis=0)

    def finish_owned(half):
        for index in FIRST:
            moves[last, half][index].wait_recv()
        x0, y0 = got_x[last, half, 0], got_y[last, half, 0]
        corner = x0[44:55] + y0[44:55] + got_corner[last, half, 0]
        return set_last(half, OWNED, (corner, x0[0:44], y0[0:44]))

    def start_others(indices):
        for half in range(2):
            for index in indices:
                moves[last, half][index].start()

    def finish_others():
        for half in range(2):
            for index, move in enumerate(moves[last, half]):
                if index not in FIRST:
                    move.wait_recv()
            x0, x5 = got_x[last, half, 0], got_x[last, half, 1]
            y0, y5 = got_y[last, half, 0], got_y[last, half, 1]
            corners = [got_corner[last, half, i] for i in range(4)]
            pair = jnp.concatenate(
                [x0[55:66] + y5[44:55] + corners[2], x5[55:66] + y5[55:66] + corners[3]], axis=0
            )
            corner = x5[44:55] + y0[55:66] + corners[1]
            set_last(half, OTHERS, (corner, pair, x5[0:44], y5[0:44]))

    rims = [finish_owned(half) for half in range(2)]
    rim_weight = jnp.concatenate([weight[rows] for rows in OWNED], axis=0)
    rim_grams = gram(jnp.concatenate(rims, axis=1), rim_weight)
    grams = tuple(a + b for a, b in zip(grams, rim_grams))
    return grams, sum(moves.values(), []), start_others, finish_others


def spread_rows(states, padded, spread):
    padded[...] = jnp.zeros(padded.shape, F32)
    for (x, y), (start, _) in COLUMNS.items():
        for half in range(2):
            padded[half, pl.ds(88 * x + y, 11, stride=8)] = states[half, start : start + 11]
    for half in range(2):
        lanes = slice(128 * half, 128 * half + 128)
        high, low = split(padded[half])
        spread[0, :, lanes] = high
        spread[1, :, lanes] = low


def rotate_phase(spread, factor, out):
    factor_high, factor_low = split(factor)
    result = dot(spread[0], factor_high) + (
        dot(spread[0], factor_low) + dot(spread[1], factor_high)
    )
    for x in range(6):
        for z in range(11):
            low = 8 * (11 * x + z)
            out[x, z] = result[low : low + 6].astype(BF16)


def fused_kernel(sizes, node_total, *refs):
    inputs, out, scratch, extra = refs[:5], refs[5], refs[6:28], refs[28:]
    (spread, own, row_in, part, column_in, whole,
     row_send, row_recv, col_send, col_recv, all_send, all_recv) = extra
    n_gx, n_gy = sizes
    my_y = lax.axis_index("gy")
    ready = greet(
        sizes,
        HALO_OFFSETS + [(0, d) for d in range(1, n_gy)] + [(d, 0) for d in range(1, n_gx)],
    )
    grams, moves, start_others, finish_others = filter_phase(sizes, inputs, scratch, ready)
    pieces, height = own.shape[0], own.shape[2] - 1
    packed, diagonal = pack(grams)
    row_moves, col_moves, all_moves = [], [], []
    for p in range(pieces):
        for index in range(n_gy):
            low = (index * pieces + p) * height
            own[p, index, 0:height] = packed[low : low + height]
            own[p, index, height : height + 1] = diagonal
        row_moves.append([
            remote(sizes, own.at[p, lax.rem(my_y + d, n_gy)], row_in.at[p, d - 1],
                   row_send.at[p, d - 1], row_recv.at[p, d - 1], (0, d))
            for d in range(1, n_gy)
        ])
        for move in row_moves[p]:
            move.start()
        if p == pieces - 1:
            start_others((0, 1, 2, 4))
        col_moves.append([
            remote(sizes, part.at[p], column_in.at[p, d - 1],
                   col_send.at[p, d - 1], col_recv.at[p, d - 1], (d, 0))
            for d in range(1, n_gx)
        ])
        all_moves.append([
            remote(sizes, whole.at[p, my_y], whole.at[p, my_y],
                   all_send.at[p, d - 1], all_recv.at[p, d - 1], (0, d))
            for d in range(1, n_gy)
        ])

    def second(p):
        for move in row_moves[p]:
            move.wait_recv()
        total = own[p, my_y]
        for d in range(1, n_gy):
            total = total + row_in[p, d - 1]
        part[p] = total
        for move in col_moves[p]:
            move.start()

    def third(p):
        for move in col_moves[p]:
            move.wait_recv()
        total = part[p]
        for d in range(1, n_gx):
            total = total + column_in[p, d - 1]
        whole[p, my_y] = total
        for move in all_moves[p]:
            move.start()

    for p in range(pieces):
        second(p)
        if p >= 1:
            third(p - 1)
    start_others((6,))
    third(pieces - 1)
    finish_others()
    spread_rows(scratch[9].at[FILTER_DEG], scratch[5], spread)
    for move in moves + sum(row_moves + col_moves, []):
        move.wait_send()
    for p in range(pieces):
        for move in all_moves[p]:
            move.wait_recv()
    for move in sum(all_moves, []):
        move.wait_send()
    packed = jnp.concatenate(
        [whole[p, index, 0:height] for index in range(n_gy) for p in range(pieces)], axis=0
    )
    factor = inverse_root(unpack(packed, whole[0, 0, height : height + 1]), node_total)
    rotate_phase(spread, factor, out)


def filter_kernel(sizes, *refs):
    inputs, filtered, stacked, scratch = refs[:5], refs[5], refs[6], refs[7:]
    grams, moves, start_others, finish_others = filter_phase(
        sizes, inputs, scratch, greet(sizes, HALO_OFFSETS)
    )
    start_others((0, 1, 2, 4, 6))
    finish_others()
    stacked[...] = jnp.concatenate(grams, axis=0)
    filtered[...] = scratch[9][FILTER_DEG]
    for move in moves:
        move.wait_send()


def rotate_kernel(node_total, filtered, stacked, out, padded, spread):
    spread_rows(filtered, padded, spread)
    total = whole_gram(stacked[0:128], stacked[128:256], stacked[256:384])
    rotate_phase(spread, inverse_root(total, node_total), out)


def body(orbitals, masses, cell_matrices):
    n_gx, n_gy = lax.axis_size("gx"), lax.axis_size("gy")
    sizes = (n_gx, n_gy)
    assert n_gy % 2 == 0
    assert orbitals.shape == (6, 6, 11, 256) and cell_matrices.shape == (1, 1, 2, 216, 216)
    node_total = 5 * n_gx * 5 * n_gy * 11
    nodes = jnp.transpose(orbitals, (0, 2, 1, 3))
    down, along = tables()
    arguments = (nodes, masses, cell_matrices, jnp.asarray(down), jnp.asarray(along))
    arguments = tuple(pltpu.with_memory_space_constraint(a, pltpu.HBM) for a in arguments)
    vmem = pl.BlockSpec(memory_space=pltpu.VMEM)
    hbm = pl.BlockSpec(memory_space=pltpu.MemorySpace.HBM)
    filter_scratch = [
        pltpu.VMEM(nodes.shape, BF16),
        pltpu.VMEM(masses.shape, F32),
        pltpu.VMEM(cell_matrices.shape, BF16),
        pltpu.VMEM(down.shape, jnp.int32),
        pltpu.VMEM(along.shape, jnp.int32),
        pltpu.VMEM((2, 528, 128), F32),
        pltpu.VMEM((48, 128), F32),
        pltpu.VMEM((ROWS, RIM), BF16),
        pltpu.VMEM((ROWS, INNER), BF16),
        pltpu.VMEM((FILTER_DEG + 1, 2, ROWS, 128), F32),
        pltpu.VMEM((2, RIM, 128), BF16),
        pltpu.VMEM((2, INNER, 128), BF16),
        pltpu.VMEM((FILTER_DEG, 2, RIM, 128), F32),
    ]
    filter_scratch += [
        pltpu.VMEM((FILTER_DEG, 2) + shape + (128,), F32)
        for shape in ((2, 66), (2, 66), (4, 11)) * 2
    ]
    filter_scratch += [
        pltpu.SemaphoreType.DMA((5,)),
        pltpu.SemaphoreType.DMA((FILTER_DEG, 2, len(MESSAGES))),
        pltpu.SemaphoreType.DMA((FILTER_DEG, 2, len(MESSAGES))),
    ]
    params = pltpu.CompilerParams(
        collective_id=0, has_side_effects=True, vmem_limit_bytes=VMEM_BYTES
    )
    if 256 % (8 * PIECES * n_gy) == 0:
        height = 256 // n_gy // PIECES + 1
        result = pl.pallas_call(
            functools.partial(fused_kernel, sizes, node_total),
            out_shape=pltpu.VMEM(nodes.shape, BF16),
            in_specs=[hbm] * 5,
            out_specs=vmem,
            scratch_shapes=filter_scratch
            + [
                pltpu.VMEM((2, 528, 256), BF16),
                pltpu.VMEM((PIECES, n_gy, height, 128), F32),
                pltpu.VMEM((PIECES, n_gy - 1, height, 128), F32),
                pltpu.VMEM((PIECES, height, 128), F32),
                pltpu.VMEM((PIECES, n_gx - 1, height, 128), F32),
                pltpu.VMEM((PIECES, n_gy, height, 128), F32),
            ]
            + [pltpu.SemaphoreType.DMA((PIECES, n - 1)) for n in (n_gy, n_gy, n_gx, n_gx, n_gy, n_gy)],
            compiler_params=params,
        )(*arguments)
    else:
        filtered, stacked = pl.pallas_call(
            functools.partial(filter_kernel, sizes),
            out_shape=[
                jax.ShapeDtypeStruct((2, ROWS, 128), F32),
                jax.ShapeDtypeStruct((384, 128), F32),
            ],
            in_specs=[hbm] * 5,
            out_specs=[vmem] * 2,
            scratch_shapes=filter_scratch,
            compiler_params=params,
        )(*arguments)
        stacked = lax.psum(stacked, ("gx", "gy"))
        result = pl.pallas_call(
            functools.partial(rotate_kernel, node_total),
            out_shape=jax.ShapeDtypeStruct(nodes.shape, BF16),
            in_specs=[vmem] * 2,
            out_specs=vmem,
            scratch_shapes=[pltpu.VMEM((2, 528, 128), F32), pltpu.VMEM((2, 528, 256), BF16)],
            compiler_params=pltpu.CompilerParams(vmem_limit_bytes=VMEM_BYTES),
        )(filtered, stacked)
    return jnp.transpose(result, (0, 2, 1, 3))


def solution(mesh):
    return jax.shard_map(
        body,
        mesh=mesh,
        in_specs=(P("gx", "gy", None, None), P("gx", "gy", None), P("gx", "gy", None, None, None)),
        out_specs=P("gx", "gy", None, None),
        check_vma=False,
    )
```

```python
import functools

import jax
import jax.numpy as jnp
import numpy as np
from jax import lax
from jax.experimental import pallas as pl
from jax.experimental.pallas import tpu as pltpu
from jax.sharding import PartitionSpec as P

FILTER_DEG = 3
CENTER_SHIFT = 12.0
HALF_SPAN = 12.0

RIM = 240
ROWS = 432
INNER = ROWS - RIM
PIECES = 1
VMEM_BYTES = 24 << 20
BF16 = jnp.bfloat16
F32 = jnp.float32

MESSAGES = (
    (-1, -1, "corner", 0, 3),
    (1, -1, "corner", 1, 2),
    (-1, 1, "corner", 2, 1),
    (1, 1, "corner", 3, 0),
    (-1, 0, "x", 0, 1),
    (1, 0, "x", 1, 0),
    (0, -1, "y", 0, 1),
    (0, 1, "y", 1, 0),
)


PAIRS = (0, 24)
X_FACES, Y_FACES = (48, 96), (144, 192)
GROUPS = tuple((start, 2) for start in PAIRS) + tuple((start, 4) for start in X_FACES + Y_FACES)
GROUPS += ((RIM, 16),)


def column_rows():
    rows = {}

    def add(columns, start):
        for i, column in enumerate(columns):
            rows[column] = (start + 11 * i, start + 11 * len(columns) + i)

    for face in range(2):
        add([(0, 5 * face), (5, 5 * face)], PAIRS[face])
        add([(5 * face, i + 1) for i in range(4)], X_FACES[face])
        add([(i + 1, 5 * face) for i in range(4)], Y_FACES[face])
    add([(i + 1, j + 1) for i in range(4) for j in range(4)], RIM)
    return rows


COLUMNS = column_rows()
FIRST = (3, 5, 7)
ORDER = tuple(("corner", i, j) for j in range(2) for i in range(2))
ORDER += tuple(("x", i, 0) for i in range(2)) + tuple(("y", 0, j) for j in range(2))
OWNED = (slice(0, 24), slice(48, 96), slice(144, 192))
OTHERS = (slice(11, 22), slice(24, 46), slice(96, 140), slice(192, 236))


def tables():
    down = np.zeros((ROWS, 128), np.int32)
    along = np.full((8, ROWS), -1, np.int32)
    for (x, y), (start, double) in COLUMNS.items():
        for z, row in [(z, start + z) for z in range(11)] + [(5, double)]:
            for cell in range(2):
                inside = 0 <= z - 5 * cell <= 5
                down[row, cell] = (x * 6 + y) * 6 + z - 5 * cell if inside else -1
            down[row, 2], down[row, 3] = 8 * x + y, z
            down[row, 4] = int(x < 5 and y < 5 and row != double)
            half = int(z > 5 or row == double)
            along[half, row] = (x * 6 + y) * 6 + z - 5 * half
    return down, along


def dot(a, b):
    return jnp.dot(a, b, preferred_element_type=F32)


def dot_rows(a, b):
    return lax.dot_general(a, b, (((0,), (0,)), ((), ())), preferred_element_type=F32)


def split(a):
    high = a.astype(BF16)
    return high, (a - high.astype(F32)).astype(BF16)


def dot3(a, b):
    a_high, a_low = split(a)
    b_high, b_low = split(b)
    return dot(a_high, b_high) + (dot(a_high, b_low) + dot(a_low, b_high))


def one_hot(condition):
    return jnp.where(condition, 1.0, 0.0).astype(F32)


def halves(rows, weight):
    return split(rows * weight) + split(rows)


def gram_first(first):
    left_high, left_low, high, low = first
    return dot_rows(left_high, high) + (dot_rows(left_high, low) + dot_rows(left_low, high))


def gram_second(first, second):
    left_high, left_low = second[:2]
    high, low = (jnp.concatenate([first[k], second[k]], axis=1) for k in (2, 3))
    both = dot_rows(left_high, high) + (dot_rows(left_high, low) + dot_rows(left_low, high))
    return both[:, :128], both[:, 128:]


def block_ids():
    return (
        lax.broadcasted_iota(jnp.int32, (128, 128), 0),
        lax.broadcasted_iota(jnp.int32, (128, 128), 1),
    )


def pack(grams):
    s00, s10, s11 = grams
    row, col = block_ids()
    diagonal = jnp.sum(jnp.where(row == col, s11, 0.0), axis=0, keepdims=True)
    return jnp.concatenate([s10, jnp.where(row <= col, s00, s11)], axis=0), diagonal


def unpack(packed, diagonal):
    s10, both = packed[0:128], packed[128:256]
    turned = both.T
    row, col = block_ids()
    s00 = jnp.where(row <= col, both, turned)
    s11 = jnp.where(row > col, both, jnp.where(row < col, turned, diagonal))
    return whole_gram(s00, s10, s11)


def whole_gram(s00, s10, s11):
    top = jnp.concatenate([s00, s10.T], axis=1)
    bottom = jnp.concatenate([s10, s11], axis=1)
    return jnp.concatenate([top, bottom], axis=0)


def inverse_root(gram_sum, node_total):
    inter = gram_sum * (1.0 / node_total)
    inter2 = dot3(inter, inter)
    frob2 = jnp.sum(jnp.sum(inter * inter, axis=0, keepdims=True), axis=1, keepdims=True)
    frob = jnp.sqrt(frob2)
    over = 1.0 / frob
    current = inter * over
    square = (inter2 * over) * over
    row_id = lax.broadcasted_iota(jnp.int32, (256, 256), 0)
    col_id = lax.broadcasted_iota(jnp.int32, (256, 256), 1)
    identity = one_hot(row_id == col_id)
    tail = 0.0625 * square - 0.5625 * current
    factor_z = 2.25 * identity - 2.4375 * current + 1.6875 * square
    factor_z = factor_z + dot(square.astype(BF16), tail.astype(BF16))
    return factor_z * (1.0 / jnp.sqrt(frob))


PLACES = {}


def at_offset(sizes, offset):
    if not all(isinstance(d, int) for d in offset):
        return place(sizes, offset)
    key = (offset[0] % sizes[0], offset[1] % sizes[1])
    if key not in PLACES:
        PLACES[key] = place(sizes, offset)
    return PLACES[key]


def place(sizes, offset):
    n_gx, n_gy = sizes
    return (
        lax.rem(lax.axis_index("gx") + (offset[0] + n_gx), n_gx),
        lax.rem(lax.axis_index("gy") + (offset[1] + n_gy), n_gy),
    )


def remote(sizes, src, dst, send, recv, offset):
    return pltpu.make_async_remote_copy(
        src_ref=src, dst_ref=dst, send_sem=send, recv_sem=recv,
        device_id=at_offset(sizes, offset), device_id_type=pl.DeviceIdType.MESH,
    )


def greet(sizes, offsets):
    PLACES.clear()
    barrier = pltpu.get_barrier_semaphore()
    offsets = sorted({(dx % sizes[0], dy % sizes[1]) for dx, dy in offsets})
    for offset in offsets:
        pl.semaphore_signal(
            barrier, inc=1, device_id=at_offset(sizes, offset),
            device_id_type=pl.DeviceIdType.MESH,
        )
    return lambda: pl.semaphore_wait(barrier, len(offsets))


HALO_OFFSETS = [(dx, dy) for dx, dy, _, _, _ in MESSAGES]


def filter_phase(sizes, inputs, scratch, ready):
    (nodes_in, masses_in, cells_in, down_in, along_in) = inputs
    (nodes, masses, cells, down, along, padded, mass_pad, rim_matrix, inner_matrix, states,
     rim_rounded, inner_rounded, sums, sent_x, sent_y, sent_corner, got_x, got_y, got_corner,
     load_sems, send_sems, recv_sems) = scratch
    last = FILTER_DEG - 1

    loads = [
        pltpu.make_async_copy(src, dst, load_sems.at[index])
        for index, (src, dst) in enumerate(
            [(down_in, down), (along_in, along), (cells_in, cells), (nodes_in, nodes),
             (masses_in, masses)]
        )
    ]
    for load in loads:
        load.start()
    loads[0].wait()
    loads[1].wait()

    rim, inner = slice(0, RIM), slice(RIM, ROWS)
    places = lax.broadcasted_iota(jnp.int32, (216, ROWS), 0)
    to_columns = [one_hot(places == along[c : c + 1, :]).astype(BF16) for c in range(2)]

    def arrange(rows):
        lanes = lax.broadcasted_iota(jnp.int32, (rows.stop - rows.start, 216), 1)
        parts = []
        for c in range(2):
            to_rows = one_hot(lanes == down[rows, c : c + 1]).astype(BF16)
            parts.append(dot(dot(to_rows, cells[0, 0, c]).astype(BF16), to_columns[c]))
        matrix = (parts[0] + parts[1]).astype(BF16)
        rim_matrix[rows] = matrix[:, :RIM]
        inner_matrix[rows] = matrix[:, RIM:]

    loads[2].wait()
    arrange(rim)

    loads[3].wait()

    def load_states(half):
        for x in range(6):
            for z in range(11):
                padded[half, 8 * (11 * x + z) : 8 * (11 * x + z) + 6] = nodes[
                    x, z, :, 128 * half : 128 * half + 128
                ].astype(F32)
        for (x, y), (start, _) in COLUMNS.items():
            states[0, half, start : start + 11] = padded[half, pl.ds(88 * x + y, 11, stride=8)]
        for start, count in GROUPS:
            states[0, half, start + 11 * count : start + 12 * count] = states[
                0, half, pl.ds(start + 5, count, stride=11)
            ]
        rim_rounded[half] = states[0, half, rim].astype(BF16)
        inner_rounded[half] = states[0, half, inner].astype(BF16)

    def load_masses():
        mass_pad[...] = jnp.zeros(mass_pad.shape, F32)
        for x in range(6):
            high, rest = split(masses[x])
            low, least = split(masses[x] - high.astype(F32))
            mass_pad[8 * x : 8 * x + 6, 0:11] = high.astype(F32)
            mass_pad[8 * x : 8 * x + 6, 16:27] = low.astype(F32)
            mass_pad[8 * x : 8 * x + 6, 32:43] = least.astype(F32)
        pick = one_hot(lax.broadcasted_iota(jnp.int32, (ROWS, 48), 1) == down[:, 2:3]).astype(BF16)
        spread = dot(pick, mass_pad[...].astype(BF16))
        lane = lax.broadcasted_iota(jnp.int32, (ROWS, 128), 1)
        return jnp.sum(
            jnp.where(lane % 16 == down[:, 3:4], spread, 0.0), axis=1, keepdims=True
        )

    side = lax.rem(lax.axis_index("gy"), 2)

    def pick(here, there):
        return jnp.where(side == 0, here, there)

    buffers = {"x": (sent_x, got_x), "y": (sent_y, got_y), "corner": (sent_corner, got_corner)}

    def moves_of(step, half):
        return [
            remote(
                sizes, buffers[kind][0].at[step, half, here], buffers[kind][1].at[step, half, there],
                send_sems.at[step, half, index], recv_sems.at[step, half, index], (dx, dy),
            )
            for index, (dx, dy, kind, here, there) in enumerate(MESSAGES)
        ]

    def advance(step, half, product, rows):
        if step == 0:
            return product * scale1[rows] - shift * states[0, half, rows]
        return (
            (2.0 * product) * scale1[rows]
            - (2.0 * shift) * states[step, half, rows]
            - states[step - 1, half, rows]
        )

    turn = lax.rem(lax.axis_index("gy"), 2)

    def ordered_moves(step, half):
        moves = []
        for kind, i, j in ORDER:
            f, g = turn + i * (1 - 2 * turn), turn + j * (1 - 2 * turn)
            here, slot, count, offset = {
                "corner": (f + 2 * g, f + 2 * g, 4, (2 * f - 1, 2 * g - 1)),
                "x": (f, 4 + f, 2, (2 * f - 1, 0)),
                "y": (g, 6 + g, 2, (0, 2 * g - 1)),
            }[kind]
            moves.append(
                remote(
                    sizes, buffers[kind][0].at[step, half, here],
                    buffers[kind][1].at[step, half, count - 1 - here],
                    send_sems.at[step, half, slot], recv_sems.at[step, half, slot], offset,
                )
            )
        return moves

    moves = {}

    def launch(step, half, ahead):
        moves[step, half] = moves_of(step, half)
        order = [moves[step, half][i] for i in FIRST] if step == last else ordered_moves(step, half)
        first = 1 if step == last else 4
        pair_rows, face_rows = slice(0, X_FACES[0]), slice(X_FACES[0], RIM)
        product = ahead[pair_rows] + dot(rim_matrix[pair_rows], rim_rounded[half])
        sums[step, half, pair_rows] = product
        pairs = [product[start : start + 22] for start in PAIRS]
        for g in range(2):
            for f in range(2):
                sent_corner[step, half, f + 2 * g] = pairs[g][11 * f : 11 * f + 11]
        if step == 0 and half == 0:
            ready()
        for move in order[:first]:
            move.start()
        product = ahead[face_rows] + dot(rim_matrix[face_rows], rim_rounded[half])
        sums[step, half, face_rows] = product
        for f in range(2):
            low = slice(11 * f, 11 * f + 11)
            x_face = product[X_FACES[f] - X_FACES[0] :][:44]
            y_face = product[Y_FACES[f] - X_FACES[0] :][:44]
            sent_x[step, half, f] = jnp.concatenate([x_face, pairs[0][low], pairs[1][low]], axis=0)
            sent_y[step, half, f] = jnp.concatenate([y_face, pairs[f]], axis=0)
        for move in order[first:]:
            move.start()

    def inside(step, half):
        inner_next = advance(
            step,
            half,
            dot(rim_matrix[inner], rim_rounded[half])
            + dot(inner_matrix[inner], inner_rounded[half]),
            inner,
        )
        states[step + 1, half, inner] = inner_next
        if step == FILTER_DEG - 1:
            return inner_next
        inner_rounded[half] = inner_next.astype(BF16)
        return dot(inner_matrix[rim], inner_rounded[half])

    def finish(step, half):
        for move in moves[step, half]:
            move.wait_recv()
        theirs = []
        for g in range(2):
            low = slice(44 + 11 * g, 55 + 11 * g)
            pair = got_y[step, half, g, 44:66] + jnp.concatenate(
                [got_x[step, half, f, low] + got_corner[step, half, f + 2 * g] for f in range(2)],
                axis=0,
            )
            theirs += [pair, pair[5:6], pair[16:17]]
        for got in (got_x, got_y):
            for f in range(2):
                theirs += [
                    got[step, half, f, 0:44],
                    got[step, half, f, pl.ds(5, 4, stride=11)],
                ]
        rim_next = advance(
            step, half, sums[step, half] + jnp.concatenate(theirs, axis=0), rim
        )
        states[step + 1, half, rim] = rim_next
        rim_rounded[half] = rim_next.astype(BF16)

    for half in range(2):
        load_states(half)
        launch(0, half, dot(inner_matrix[rim], inner_rounded[half]))
    arrange(inner)
    loads[4].wait()
    mass = load_masses()
    weight = mass * down[:, 4:5].astype(F32)
    scale1 = 1.0 / (HALF_SPAN * mass)
    shift = CENTER_SHIFT / HALF_SPAN
    ahead = [inside(0, half) for half in range(2)]
    for step in range(last):
        for half in range(2):
            finish(step, half)
            launch(step + 1, half, ahead[half])
            ahead[half] = inside(step + 1, half)
    parts = [halves(a, weight[inner]) for a in ahead]
    grams = (gram_first(parts[0]),) + gram_second(*parts)

    def set_last(half, groups, theirs):
        values = []
        for rows, their in zip(groups, theirs):
            values.append(advance(last, half, sums[last, half, rows] + their, rows))
            states[last + 1, half, rows] = values[-1]
        return jnp.concatenate(values, axis=0)

    def finish_owned(half):
        for index in FIRST:
            moves[last, half][index].wait_recv()
        x0, y0 = got_x[last, half, 0], got_y[last, half, 0]
        corner = x0[44:55] + y0[44:55] + got_corner[last, half, 0]
        theirs = [
            jnp.concatenate([a, jnp.zeros((rows.stop - rows.start - a.shape[0], 128), F32)], axis=0)
            for rows, a in zip(OWNED, (corner, x0[0:44], y0[0:44]))
        ]
        return set_last(half, OWNED, theirs)

    def start_others(indices):
        for half in range(2):
            for index in indices:
                moves[last, half][index].start()

    def finish_others():
        for half in range(2):
            for index, move in enumerate(moves[last, half]):
                if index not in FIRST:
                    move.wait_recv()
            x0, x5 = got_x[last, half, 0], got_x[last, half, 1]
            y0, y5 = got_y[last, half, 0], got_y[last, half, 1]
            corners = [got_corner[last, half, i] for i in range(4)]
            pair = jnp.concatenate(
                [x0[55:66] + y5[44:55] + corners[2], x5[55:66] + y5[55:66] + corners[3]], axis=0
            )
            corner = x5[44:55] + y0[55:66] + corners[1]
            set_last(half, OTHERS, (corner, pair, x5[0:44], y5[0:44]))

    rim_weight = jnp.concatenate([weight[rows] for rows in OWNED], axis=0)
    first = halves(finish_owned(0), rim_weight)
    s00 = grams[0] + gram_first(first)
    s10, s11 = gram_second(first, halves(finish_owned(1), rim_weight))
    grams = (s00, grams[1] + s10, grams[2] + s11)
    return grams, sum(moves.values(), []), start_others, finish_others


def spread_rows(states, padded, spread):
    padded[...] = jnp.zeros(padded.shape, F32)
    for (x, y), (start, _) in COLUMNS.items():
        for half in range(2):
            padded[half, pl.ds(88 * x + y, 11, stride=8)] = states[half, start : start + 11]
    for half in range(2):
        lanes = slice(128 * half, 128 * half + 128)
        high, low = split(padded[half])
        spread[0, :, lanes] = high
        spread[1, :, lanes] = low


def rotate_phase(spread, factor, out):
    factor_high, factor_low = split(factor)
    result = dot(spread[0], factor_high) + (
        dot(spread[0], factor_low) + dot(spread[1], factor_high)
    )
    for x in range(6):
        for z in range(11):
            low = 8 * (11 * x + z)
            out[x, z] = result[low : low + 6].astype(BF16)


def fused_kernel(sizes, node_total, *refs):
    inputs, out, scratch, extra = refs[:5], refs[5], refs[6:28], refs[28:]
    (spread, own, row_in, part, column_in, whole,
     row_send, row_recv, col_send, col_recv, all_send, all_recv) = extra
    n_gx, n_gy = sizes
    my_y = lax.axis_index("gy")
    ready = greet(
        sizes,
        HALO_OFFSETS + [(0, d) for d in range(1, n_gy)] + [(d, 0) for d in range(1, n_gx)],
    )
    grams, moves, start_others, finish_others = filter_phase(sizes, inputs, scratch, ready)
    pieces, height = own.shape[0], own.shape[2] - 1
    packed, diagonal = pack(grams)
    row_moves, col_moves, all_moves = [], [], []
    for p in range(pieces):
        for index in range(n_gy):
            low = (index * pieces + p) * height
            own[p, index, 0:height] = packed[low : low + height]
            own[p, index, height : height + 1] = diagonal
        row_moves.append([
            remote(sizes, own.at[p, lax.rem(my_y + d, n_gy)], row_in.at[p, d - 1],
                   row_send.at[p, d - 1], row_recv.at[p, d - 1], (0, d))
            for d in range(1, n_gy)
        ])
        for move in row_moves[p]:
            move.start()
        if p == pieces - 1:
            start_others((0, 1, 2, 4))
        col_moves.append([
            remote(sizes, part.at[p], column_in.at[p, d - 1],
                   col_send.at[p, d - 1], col_recv.at[p, d - 1], (d, 0))
            for d in range(1, n_gx)
        ])
        all_moves.append([
            remote(sizes, whole.at[p, my_y], whole.at[p, my_y],
                   all_send.at[p, d - 1], all_recv.at[p, d - 1], (0, d))
            for d in range(1, n_gy)
        ])

    def second(p):
        for move in row_moves[p]:
            move.wait_recv()
        total = own[p, my_y]
        for d in range(1, n_gy):
            total = total + row_in[p, d - 1]
        part[p] = total
        for move in col_moves[p]:
            move.start()

    def third(p):
        for move in col_moves[p]:
            move.wait_recv()
        total = part[p]
        for d in range(1, n_gx):
            total = total + column_in[p, d - 1]
        whole[p, my_y] = total
        for move in all_moves[p]:
            move.start()

    for p in range(pieces):
        second(p)
        if p >= 1:
            third(p - 1)
    start_others((6,))
    third(pieces - 1)
    finish_others()
    spread_rows(scratch[9].at[FILTER_DEG], scratch[5], spread)
    for move in moves + sum(row_moves + col_moves, []):
        move.wait_send()
    for p in range(pieces):
        for move in all_moves[p]:
            move.wait_recv()
    for move in sum(all_moves, []):
        move.wait_send()
    packed = jnp.concatenate(
        [whole[p, index, 0:height] for index in range(n_gy) for p in range(pieces)], axis=0
    )
    factor = inverse_root(unpack(packed, whole[0, 0, height : height + 1]), node_total)
    rotate_phase(spread, factor, out)


def filter_kernel(sizes, *refs):
    inputs, filtered, stacked, scratch = refs[:5], refs[5], refs[6], refs[7:]
    grams, moves, start_others, finish_others = filter_phase(
        sizes, inputs, scratch, greet(sizes, HALO_OFFSETS)
    )
    start_others((0, 1, 2, 4, 6))
    finish_others()
    stacked[...] = jnp.concatenate(grams, axis=0)
    filtered[...] = scratch[9][FILTER_DEG]
    for move in moves:
        move.wait_send()


def rotate_kernel(node_total, filtered, stacked, out, padded, spread):
    spread_rows(filtered, padded, spread)
    total = whole_gram(stacked[0:128], stacked[128:256], stacked[256:384])
    rotate_phase(spread, inverse_root(total, node_total), out)


def body(orbitals, masses, cell_matrices):
    n_gx, n_gy = lax.axis_size("gx"), lax.axis_size("gy")
    sizes = (n_gx, n_gy)
    assert n_gy % 2 == 0
    assert orbitals.shape == (6, 6, 11, 256) and cell_matrices.shape == (1, 1, 2, 216, 216)
    node_total = 5 * n_gx * 5 * n_gy * 11
    nodes = jnp.transpose(orbitals, (0, 2, 1, 3))
    down, along = tables()
    arguments = (nodes, masses, cell_matrices, jnp.asarray(down), jnp.asarray(along))
    arguments = tuple(pltpu.with_memory_space_constraint(a, pltpu.HBM) for a in arguments)
    vmem = pl.BlockSpec(memory_space=pltpu.VMEM)
    hbm = pl.BlockSpec(memory_space=pltpu.MemorySpace.HBM)
    filter_scratch = [
        pltpu.VMEM(nodes.shape, BF16),
        pltpu.VMEM(masses.shape, F32),
        pltpu.VMEM(cell_matrices.shape, BF16),
        pltpu.VMEM(down.shape, jnp.int32),
        pltpu.VMEM(along.shape, jnp.int32),
        pltpu.VMEM((2, 528, 128), F32),
        pltpu.VMEM((48, 128), F32),
        pltpu.VMEM((ROWS, RIM), BF16),
        pltpu.VMEM((ROWS, INNER), BF16),
        pltpu.VMEM((FILTER_DEG + 1, 2, ROWS, 128), F32),
        pltpu.VMEM((2, RIM, 128), BF16),
        pltpu.VMEM((2, INNER, 128), BF16),
        pltpu.VMEM((FILTER_DEG, 2, RIM, 128), F32),
    ]
    filter_scratch += [
        pltpu.VMEM((FILTER_DEG, 2) + shape + (128,), F32)
        for shape in ((2, 66), (2, 66), (4, 11)) * 2
    ]
    filter_scratch += [
        pltpu.SemaphoreType.DMA((5,)),
        pltpu.SemaphoreType.DMA((FILTER_DEG, 2, len(MESSAGES))),
        pltpu.SemaphoreType.DMA((FILTER_DEG, 2, len(MESSAGES))),
    ]
    params = pltpu.CompilerParams(
        collective_id=0, has_side_effects=True, vmem_limit_bytes=VMEM_BYTES
    )
    if 256 % (8 * PIECES * n_gy) == 0:
        height = 256 // n_gy // PIECES + 1
        result = pl.pallas_call(
            functools.partial(fused_kernel, sizes, node_total),
            out_shape=pltpu.VMEM(nodes.shape, BF16),
            in_specs=[hbm] * 5,
            out_specs=vmem,
            scratch_shapes=filter_scratch
            + [
                pltpu.VMEM((2, 528, 256), BF16),
                pltpu.VMEM((PIECES, n_gy, height, 128), F32),
                pltpu.VMEM((PIECES, n_gy - 1, height, 128), F32),
                pltpu.VMEM((PIECES, height, 128), F32),
                pltpu.VMEM((PIECES, n_gx - 1, height, 128), F32),
                pltpu.VMEM((PIECES, n_gy, height, 128), F32),
            ]
            + [pltpu.SemaphoreType.DMA((PIECES, n - 1)) for n in (n_gy, n_gy, n_gx, n_gx, n_gy, n_gy)],
            compiler_params=params,
        )(*arguments)
    else:
        filtered, stacked = pl.pallas_call(
            functools.partial(filter_kernel, sizes),
            out_shape=[
                jax.ShapeDtypeStruct((2, ROWS, 128), F32),
                jax.ShapeDtypeStruct((384, 128), F32),
            ],
            in_specs=[hbm] * 5,
            out_specs=[vmem] * 2,
            scratch_shapes=filter_scratch,
            compiler_params=params,
        )(*arguments)
        stacked = lax.psum(stacked, ("gx", "gy"))
        result = pl.pallas_call(
            functools.partial(rotate_kernel, node_total),
            out_shape=jax.ShapeDtypeStruct(nodes.shape, BF16),
            in_specs=[vmem] * 2,
            out_specs=vmem,
            scratch_shapes=[pltpu.VMEM((2, 528, 128), F32), pltpu.VMEM((2, 528, 256), BF16)],
            compiler_params=pltpu.CompilerParams(vmem_limit_bytes=VMEM_BYTES),
        )(filtered, stacked)
    return jnp.transpose(result, (0, 2, 1, 3))


def solution(mesh):
    return jax.shard_map(
        body,
        mesh=mesh,
        in_specs=(P("gx", "gy", None, None), P("gx", "gy", None), P("gx", "gy", None, None, None)),
        out_specs=P("gx", "gy", None, None),
        check_vma=False,
    )
```

```python
import functools

import jax
import jax.numpy as jnp
import numpy as np
from jax import lax
from jax.experimental import pallas as pl
from jax.experimental.pallas import tpu as pltpu
from jax.sharding import PartitionSpec as P

FILTER_DEG = 3
CENTER_SHIFT = 12.0
HALF_SPAN = 12.0

RIM = 240
ROWS = 432
INNER = ROWS - RIM
PIECES = 1
VMEM_BYTES = 24 << 20
BF16 = jnp.bfloat16
F32 = jnp.float32

MESSAGES = (
    (-1, -1, "corner", 0, 3),
    (1, -1, "corner", 1, 2),
    (-1, 1, "corner", 2, 1),
    (1, 1, "corner", 3, 0),
    (-1, 0, "x", 0, 1),
    (1, 0, "x", 1, 0),
    (0, -1, "y", 0, 1),
    (0, 1, "y", 1, 0),
)


PAIRS = (0, 24)
X_FACES, Y_FACES = (48, 96), (144, 192)
GROUPS = tuple((start, 2) for start in PAIRS) + tuple((start, 4) for start in X_FACES + Y_FACES)
GROUPS += ((RIM, 16),)


def column_rows():
    rows = {}

    def add(columns, start):
        for i, column in enumerate(columns):
            rows[column] = (start + 11 * i, start + 11 * len(columns) + i)

    for face in range(2):
        add([(0, 5 * face), (5, 5 * face)], PAIRS[face])
        add([(5 * face, i + 1) for i in range(4)], X_FACES[face])
        add([(i + 1, 5 * face) for i in range(4)], Y_FACES[face])
    add([(i + 1, j + 1) for i in range(4) for j in range(4)], RIM)
    return rows


COLUMNS = column_rows()
FIRST = (3, 5, 7)
ORDER = tuple(("corner", i, j) for j in range(2) for i in range(2))
ORDER += tuple(("x", i, 0) for i in range(2)) + tuple(("y", 0, j) for j in range(2))
OWNED = (slice(0, 11), slice(48, 92), slice(144, 188))
OTHERS = (slice(11, 22), slice(24, 46), slice(96, 140), slice(192, 236))


def tables():
    down = np.zeros((ROWS, 128), np.int32)
    along = np.full((8, ROWS), -1, np.int32)
    for (x, y), (start, double) in COLUMNS.items():
        for z, row in [(z, start + z) for z in range(11)] + [(5, double)]:
            for cell in range(2):
                inside = 0 <= z - 5 * cell <= 5
                down[row, cell] = (x * 6 + y) * 6 + z - 5 * cell if inside else -1
            down[row, 2], down[row, 3] = 8 * x + y, z
            down[row, 4] = int(x < 5 and y < 5 and row != double)
            half = int(z > 5 or row == double)
            along[half, row] = (x * 6 + y) * 6 + z - 5 * half
    return down, along


def dot(a, b):
    return jnp.dot(a, b, preferred_element_type=F32)


def dot_rows(a, b):
    return lax.dot_general(a, b, (((0,), (0,)), ((), ())), preferred_element_type=F32)


def split(a):
    high = a.astype(BF16)
    return high, (a - high.astype(F32)).astype(BF16)


def dot3(a, b):
    a_high, a_low = split(a)
    b_high, b_low = split(b)
    return dot(a_high, b_high) + (dot(a_high, b_low) + dot(a_low, b_high))


def one_hot(condition):
    return jnp.where(condition, 1.0, 0.0).astype(F32)


def gram(rows, weight):
    a_high, a_low = split(rows * weight)
    b_high, b_low = split(rows)

    def part(lanes, columns):
        return dot_rows(a_high[:, lanes], b_high[:, columns]) + (
            dot_rows(a_high[:, lanes], b_low[:, columns])
            + dot_rows(a_low[:, lanes], b_high[:, columns])
        )

    top = part(slice(0, 128), slice(0, 256))
    return top[:, :128], top[:, 128:], part(slice(128, 256), slice(128, 256))


def block_ids():
    return (
        lax.broadcasted_iota(jnp.int32, (128, 128), 0),
        lax.broadcasted_iota(jnp.int32, (128, 128), 1),
    )


def pack(grams):
    s00, s01, s11 = grams
    row, col = block_ids()
    diagonal = jnp.sum(jnp.where(row == col, s11, 0.0), axis=0, keepdims=True)
    return jnp.concatenate([s01, jnp.where(row <= col, s00, s11)], axis=0), diagonal


def unpack(packed, diagonal):
    s01, both = packed[0:128], packed[128:256]
    turned = both.T
    row, col = block_ids()
    s00 = jnp.where(row <= col, both, turned)
    s11 = jnp.where(row > col, both, jnp.where(row < col, turned, diagonal))
    return whole_gram(s00, s01, s11)


def whole_gram(s00, s01, s11):
    top = jnp.concatenate([s00, s01], axis=1)
    bottom = jnp.concatenate([s01.T, s11], axis=1)
    return jnp.concatenate([top, bottom], axis=0)


def inverse_root(gram_sum, node_total):
    inter = gram_sum * (1.0 / node_total)
    inter2 = dot3(inter, inter)
    frob2 = jnp.sum(jnp.sum(inter * inter, axis=0, keepdims=True), axis=1, keepdims=True)
    frob = jnp.sqrt(frob2)
    over = 1.0 / frob
    current = inter * over
    square = (inter2 * over) * over
    row_id = lax.broadcasted_iota(jnp.int32, (256, 256), 0)
    col_id = lax.broadcasted_iota(jnp.int32, (256, 256), 1)
    identity = one_hot(row_id == col_id)
    tail = 0.0625 * square - 0.5625 * current
    factor_z = 2.25 * identity - 2.4375 * current + 1.6875 * square
    factor_z = factor_z + dot(square.astype(BF16), tail.astype(BF16))
    return factor_z * (1.0 / jnp.sqrt(frob))


def at_offset(sizes, offset):
    n_gx, n_gy = sizes
    return (
        lax.rem(lax.axis_index("gx") + (offset[0] + n_gx), n_gx),
        lax.rem(lax.axis_index("gy") + (offset[1] + n_gy), n_gy),
    )


def remote(sizes, src, dst, send, recv, offset):
    return pltpu.make_async_remote_copy(
        src_ref=src, dst_ref=dst, send_sem=send, recv_sem=recv,
        device_id=at_offset(sizes, offset), device_id_type=pl.DeviceIdType.MESH,
    )


def greet(sizes, offsets):
    barrier = pltpu.get_barrier_semaphore()
    offsets = sorted({(dx % sizes[0], dy % sizes[1]) for dx, dy in offsets})
    for offset in offsets:
        pl.semaphore_signal(
            barrier, inc=1, device_id=at_offset(sizes, offset),
            device_id_type=pl.DeviceIdType.MESH,
        )
    return lambda: pl.semaphore_wait(barrier, len(offsets))


HALO_OFFSETS = [(dx, dy) for dx, dy, _, _, _ in MESSAGES]


def filter_phase(sizes, inputs, scratch, ready):
    (nodes_in, masses_in, cells_in, down_in, along_in) = inputs
    (nodes, masses, cells, down, along, padded, mass_pad, rim_matrix, inner_matrix, states,
     rim_rounded, inner_rounded, sums, sent_x, sent_y, sent_corner, got_x, got_y, got_corner,
     load_sems, send_sems, recv_sems) = scratch
    last = FILTER_DEG - 1

    loads = [
        pltpu.make_async_copy(src, dst, load_sems.at[index])
        for index, (src, dst) in enumerate(
            [(down_in, down), (along_in, along), (cells_in, cells), (nodes_in, nodes),
             (masses_in, masses)]
        )
    ]
    for load in loads:
        load.start()
    loads[0].wait()
    loads[1].wait()

    rim, inner = slice(0, RIM), slice(RIM, ROWS)
    places = lax.broadcasted_iota(jnp.int32, (216, ROWS), 0)
    to_columns = [one_hot(places == along[c : c + 1, :]).astype(BF16) for c in range(2)]

    def arrange(rows):
        lanes = lax.broadcasted_iota(jnp.int32, (rows.stop - rows.start, 216), 1)
        parts = []
        for c in range(2):
            to_rows = one_hot(lanes == down[rows, c : c + 1]).astype(BF16)
            parts.append(dot(dot(to_rows, cells[0, 0, c]).astype(BF16), to_columns[c]))
        matrix = (parts[0] + parts[1]).astype(BF16)
        rim_matrix[rows] = matrix[:, :RIM]
        inner_matrix[rows] = matrix[:, RIM:]

    loads[2].wait()
    arrange(rim)

    loads[3].wait()

    def load_states(half):
        for x in range(6):
            for z in range(11):
                padded[half, 8 * (11 * x + z) : 8 * (11 * x + z) + 6] = nodes[
                    x, z, :, 128 * half : 128 * half + 128
                ].astype(F32)
        for (x, y), (start, _) in COLUMNS.items():
            states[0, half, start : start + 11] = padded[half, pl.ds(88 * x + y, 11, stride=8)]
        for start, count in GROUPS:
            states[0, half, start + 11 * count : start + 12 * count] = states[
                0, half, pl.ds(start + 5, count, stride=11)
            ]
        rim_rounded[half] = states[0, half, rim].astype(BF16)
        inner_rounded[half] = states[0, half, inner].astype(BF16)

    def load_masses():
        mass_pad[...] = jnp.zeros(mass_pad.shape, F32)
        for x in range(6):
            high, rest = split(masses[x])
            low, least = split(masses[x] - high.astype(F32))
            mass_pad[8 * x : 8 * x + 6, 0:11] = high.astype(F32)
            mass_pad[8 * x : 8 * x + 6, 16:27] = low.astype(F32)
            mass_pad[8 * x : 8 * x + 6, 32:43] = least.astype(F32)
        pick = one_hot(lax.broadcasted_iota(jnp.int32, (ROWS, 48), 1) == down[:, 2:3]).astype(BF16)
        spread = dot(pick, mass_pad[...].astype(BF16))
        lane = lax.broadcasted_iota(jnp.int32, (ROWS, 128), 1)
        return jnp.sum(
            jnp.where(lane % 16 == down[:, 3:4], spread, 0.0), axis=1, keepdims=True
        )

    side = lax.rem(lax.axis_index("gy"), 2)

    def pick(here, there):
        return jnp.where(side == 0, here, there)

    buffers = {"x": (sent_x, got_x), "y": (sent_y, got_y), "corner": (sent_corner, got_corner)}

    def moves_of(step, half):
        return [
            remote(
                sizes, buffers[kind][0].at[step, half, here], buffers[kind][1].at[step, half, there],
                send_sems.at[step, half, index], recv_sems.at[step, half, index], (dx, dy),
            )
            for index, (dx, dy, kind, here, there) in enumerate(MESSAGES)
        ]

    def advance(step, half, product, rows):
        if step == 0:
            return product * scale1[rows] - shift * states[0, half, rows]
        return (
            (2.0 * product) * scale1[rows]
            - (2.0 * shift) * states[step, half, rows]
            - states[step - 1, half, rows]
        )

    turn = lax.rem(lax.axis_index("gy"), 2)

    def ordered_moves(step, half):
        moves = []
        for kind, i, j in ORDER:
            f, g = turn + i * (1 - 2 * turn), turn + j * (1 - 2 * turn)
            here, slot, count, offset = {
                "corner": (f + 2 * g, f + 2 * g, 4, (2 * f - 1, 2 * g - 1)),
                "x": (f, 4 + f, 2, (2 * f - 1, 0)),
                "y": (g, 6 + g, 2, (0, 2 * g - 1)),
            }[kind]
            moves.append(
                remote(
                    sizes, buffers[kind][0].at[step, half, here],
                    buffers[kind][1].at[step, half, count - 1 - here],
                    send_sems.at[step, half, slot], recv_sems.at[step, half, slot], offset,
                )
            )
        return moves

    moves = {}

    def launch(step, half, ahead):
        moves[step, half] = moves_of(step, half)
        order = [moves[step, half][i] for i in FIRST] if step == last else ordered_moves(step, half)
        first = 1 if step == last else 4
        pair_rows, face_rows = slice(0, X_FACES[0]), slice(X_FACES[0], RIM)
        product = ahead[pair_rows] + dot(rim_matrix[pair_rows], rim_rounded[half])
        sums[step, half, pair_rows] = product
        pairs = [product[start : start + 22] for start in PAIRS]
        for g in range(2):
            for f in range(2):
                sent_corner[step, half, f + 2 * g] = pairs[g][11 * f : 11 * f + 11]
        if step == 0 and half == 0:
            ready()
        for move in order[:first]:
            move.start()
        product = ahead[face_rows] + dot(rim_matrix[face_rows], rim_rounded[half])
        sums[step, half, face_rows] = product
        for f in range(2):
            low = slice(11 * f, 11 * f + 11)
            x_face = product[X_FACES[f] - X_FACES[0] :][:44]
            y_face = product[Y_FACES[f] - X_FACES[0] :][:44]
            sent_x[step, half, f] = jnp.concatenate([x_face, pairs[0][low], pairs[1][low]], axis=0)
            sent_y[step, half, f] = jnp.concatenate([y_face, pairs[f]], axis=0)
        for move in order[first:]:
            move.start()

    def inside(step, half):
        inner_next = advance(
            step,
            half,
            dot(rim_matrix[inner], rim_rounded[half])
            + dot(inner_matrix[inner], inner_rounded[half]),
            inner,
        )
        states[step + 1, half, inner] = inner_next
        if step == FILTER_DEG - 1:
            return inner_next
        inner_rounded[half] = inner_next.astype(BF16)
        return dot(inner_matrix[rim], inner_rounded[half])

    def finish(step, half):
        def set_next(rows, theirs):
            their = jnp.concatenate(theirs, axis=0)
            following = advance(step, half, sums[step, half, rows] + their, rows)
            states[step + 1, half, rows] = following
            rim_rounded[half, rows] = following.astype(BF16)

        for move in moves[step, half][4:]:
            move.wait_recv()
        theirs = []
        for got in (got_x, got_y):
            for f in range(2):
                theirs += [
                    got[step, half, f, 0:44],
                    got[step, half, f, pl.ds(5, 4, stride=11)],
                ]
        set_next(slice(X_FACES[0], RIM), theirs)
        for move in moves[step, half][:4]:
            move.wait_recv()
        theirs = []
        for g in range(2):
            low = slice(44 + 11 * g, 55 + 11 * g)
            pair = got_y[step, half, g, 44:66] + jnp.concatenate(
                [got_x[step, half, f, low] + got_corner[step, half, f + 2 * g] for f in range(2)],
                axis=0,
            )
            theirs += [pair, pair[5:6], pair[16:17]]
        set_next(slice(0, X_FACES[0]), theirs)

    for half in range(2):
        load_states(half)
        launch(0, half, dot(inner_matrix[rim], inner_rounded[half]))
    arrange(inner)
    loads[4].wait()
    mass = load_masses()
    weight = mass * down[:, 4:5].astype(F32)
    scale1 = 1.0 / (HALF_SPAN * mass)
    shift = CENTER_SHIFT / HALF_SPAN
    ahead = [inside(0, half) for half in range(2)]
    for step in range(last):
        for half in range(2):
            finish(step, half)
            launch(step + 1, half, ahead[half])
            ahead[half] = inside(step + 1, half)
    grams = gram(jnp.concatenate(ahead, axis=1), weight[inner])

    def set_last(half, groups, theirs):
        values = []
        for rows, their in zip(groups, theirs):
            values.append(advance(last, half, sums[last, half, rows] + their, rows))
            states[last + 1, half, rows] = values[-1]
        return jnp.concatenate(values, axis=0)

    def finish_owned(half):
        for index in FIRST:
            moves[last, half][index].wait_recv()
        x0, y0 = got_x[last, half, 0], got_y[last, half, 0]
        corner = x0[44:55] + y0[44:55] + got_corner[last, half, 0]
        return set_last(half, OWNED, (corner, x0[0:44], y0[0:44]))

    def start_others(indices):
        for half in range(2):
            for index in indices:
                moves[last, half][index].start()

    def finish_others():
        for half in range(2):
            for index, move in enumerate(moves[last, half]):
                if index not in FIRST:
                    move.wait_recv()
            x0, x5 = got_x[last, half, 0], got_x[last, half, 1]
            y0, y5 = got_y[last, half, 0], got_y[last, half, 1]
            corners = [got_corner[last, half, i] for i in range(4)]
            pair = jnp.concatenate(
                [x0[55:66] + y5[44:55] + corners[2], x5[55:66] + y5[55:66] + corners[3]], axis=0
            )
            corner = x5[44:55] + y0[55:66] + corners[1]
            set_last(half, OTHERS, (corner, pair, x5[0:44], y5[0:44]))

    rims = [finish_owned(half) for half in range(2)]
    rim_weight = jnp.concatenate([weight[rows] for rows in OWNED], axis=0)
    rim_grams = gram(jnp.concatenate(rims, axis=1), rim_weight)
    grams = tuple(a + b for a, b in zip(grams, rim_grams))
    return grams, sum(moves.values(), []), start_others, finish_others


def spread_rows(states, padded, spread):
    padded[...] = jnp.zeros(padded.shape, F32)
    for (x, y), (start, _) in COLUMNS.items():
        for half in range(2):
            padded[half, pl.ds(88 * x + y, 11, stride=8)] = states[half, start : start + 11]
    for half in range(2):
        lanes = slice(128 * half, 128 * half + 128)
        high, low = split(padded[half])
        spread[0, :, lanes] = high
        spread[1, :, lanes] = low


def rotate_phase(spread, factor, out):
    factor_high, factor_low = split(factor)
    result = dot(spread[0], factor_high) + (
        dot(spread[0], factor_low) + dot(spread[1], factor_high)
    )
    for x in range(6):
        for z in range(11):
            low = 8 * (11 * x + z)
            out[x, z] = result[low : low + 6].astype(BF16)


def fused_kernel(sizes, node_total, *refs):
    inputs, out, scratch, extra = refs[:5], refs[5], refs[6:28], refs[28:]
    (spread, own, row_in, part, column_in, whole,
     row_send, row_recv, col_send, col_recv, all_send, all_recv) = extra
    n_gx, n_gy = sizes
    my_y = lax.axis_index("gy")
    ready = greet(
        sizes,
        HALO_OFFSETS + [(0, d) for d in range(1, n_gy)] + [(d, 0) for d in range(1, n_gx)],
    )
    grams, moves, start_others, finish_others = filter_phase(sizes, inputs, scratch, ready)
    pieces, height = own.shape[0], own.shape[2] - 1
    packed, diagonal = pack(grams)
    row_moves, col_moves, all_moves = [], [], []
    for p in range(pieces):
        for index in range(n_gy):
            low = (index * pieces + p) * height
            own[p, index, 0:height] = packed[low : low + height]
            own[p, index, height : height + 1] = diagonal
        row_moves.append([
            remote(sizes, own.at[p, lax.rem(my_y + d, n_gy)], row_in.at[p, d - 1],
                   row_send.at[p, d - 1], row_recv.at[p, d - 1], (0, d))
            for d in range(1, n_gy)
        ])
        for move in row_moves[p]:
            move.start()
        if p == pieces - 1:
            start_others((0, 1, 2, 4))
        col_moves.append([
            remote(sizes, part.at[p], column_in.at[p, d - 1],
                   col_send.at[p, d - 1], col_recv.at[p, d - 1], (d, 0))
            for d in range(1, n_gx)
        ])
        all_moves.append([
            remote(sizes, whole.at[p, my_y], whole.at[p, my_y],
                   all_send.at[p, d - 1], all_recv.at[p, d - 1], (0, d))
            for d in range(1, n_gy)
        ])

    def second(p):
        for move in row_moves[p]:
            move.wait_recv()
        total = own[p, my_y]
        for d in range(1, n_gy):
            total = total + row_in[p, d - 1]
        part[p] = total
        for move in col_moves[p]:
            move.start()

    def third(p):
        for move in col_moves[p]:
            move.wait_recv()
        total = part[p]
        for d in range(1, n_gx):
            total = total + column_in[p, d - 1]
        whole[p, my_y] = total
        for move in all_moves[p]:
            move.start()

    for p in range(pieces):
        second(p)
        if p >= 1:
            third(p - 1)
    start_others((6,))
    third(pieces - 1)
    finish_others()
    spread_rows(scratch[9].at[FILTER_DEG], scratch[5], spread)
    for move in moves + sum(row_moves + col_moves, []):
        move.wait_send()
    for p in range(pieces):
        for move in all_moves[p]:
            move.wait_recv()
    for move in sum(all_moves, []):
        move.wait_send()
    packed = jnp.concatenate(
        [whole[p, index, 0:height] for index in range(n_gy) for p in range(pieces)], axis=0
    )
    factor = inverse_root(unpack(packed, whole[0, 0, height : height + 1]), node_total)
    rotate_phase(spread, factor, out)


def filter_kernel(sizes, *refs):
    inputs, filtered, stacked, scratch = refs[:5], refs[5], refs[6], refs[7:]
    grams, moves, start_others, finish_others = filter_phase(
        sizes, inputs, scratch, greet(sizes, HALO_OFFSETS)
    )
    start_others((0, 1, 2, 4, 6))
    finish_others()
    stacked[...] = jnp.concatenate(grams, axis=0)
    filtered[...] = scratch[9][FILTER_DEG]
    for move in moves:
        move.wait_send()


def rotate_kernel(node_total, filtered, stacked, out, padded, spread):
    spread_rows(filtered, padded, spread)
    total = whole_gram(stacked[0:128], stacked[128:256], stacked[256:384])
    rotate_phase(spread, inverse_root(total, node_total), out)


def body(orbitals, masses, cell_matrices):
    n_gx, n_gy = lax.axis_size("gx"), lax.axis_size("gy")
    sizes = (n_gx, n_gy)
    assert n_gy % 2 == 0
    assert orbitals.shape == (6, 6, 11, 256) and cell_matrices.shape == (1, 1, 2, 216, 216)
    node_total = 5 * n_gx * 5 * n_gy * 11
    nodes = jnp.transpose(orbitals, (0, 2, 1, 3))
    down, along = tables()
    arguments = (nodes, masses, cell_matrices, jnp.asarray(down), jnp.asarray(along))
    arguments = tuple(pltpu.with_memory_space_constraint(a, pltpu.HBM) for a in arguments)
    vmem = pl.BlockSpec(memory_space=pltpu.VMEM)
    hbm = pl.BlockSpec(memory_space=pltpu.MemorySpace.HBM)
    filter_scratch = [
        pltpu.VMEM(nodes.shape, BF16),
        pltpu.VMEM(masses.shape, F32),
        pltpu.VMEM(cell_matrices.shape, BF16),
        pltpu.VMEM(down.shape, jnp.int32),
        pltpu.VMEM(along.shape, jnp.int32),
        pltpu.VMEM((2, 528, 128), F32),
        pltpu.VMEM((48, 128), F32),
        pltpu.VMEM((ROWS, RIM), BF16),
        pltpu.VMEM((ROWS, INNER), BF16),
        pltpu.VMEM((FILTER_DEG + 1, 2, ROWS, 128), F32),
        pltpu.VMEM((2, RIM, 128), BF16),
        pltpu.VMEM((2, INNER, 128), BF16),
        pltpu.VMEM((FILTER_DEG, 2, RIM, 128), F32),
    ]
    filter_scratch += [
        pltpu.VMEM((FILTER_DEG, 2) + shape + (128,), F32)
        for shape in ((2, 66), (2, 66), (4, 11)) * 2
    ]
    filter_scratch += [
        pltpu.SemaphoreType.DMA((5,)),
        pltpu.SemaphoreType.DMA((FILTER_DEG, 2, len(MESSAGES))),
        pltpu.SemaphoreType.DMA((FILTER_DEG, 2, len(MESSAGES))),
    ]
    params = pltpu.CompilerParams(
        collective_id=0, has_side_effects=True, vmem_limit_bytes=VMEM_BYTES
    )
    if 256 % (8 * PIECES * n_gy) == 0:
        height = 256 // n_gy // PIECES + 1
        result = pl.pallas_call(
            functools.partial(fused_kernel, sizes, node_total),
            out_shape=pltpu.VMEM(nodes.shape, BF16),
            in_specs=[hbm] * 5,
            out_specs=vmem,
            scratch_shapes=filter_scratch
            + [
                pltpu.VMEM((2, 528, 256), BF16),
                pltpu.VMEM((PIECES, n_gy, height, 128), F32),
                pltpu.VMEM((PIECES, n_gy - 1, height, 128), F32),
                pltpu.VMEM((PIECES, height, 128), F32),
                pltpu.VMEM((PIECES, n_gx - 1, height, 128), F32),
                pltpu.VMEM((PIECES, n_gy, height, 128), F32),
            ]
            + [pltpu.SemaphoreType.DMA((PIECES, n - 1)) for n in (n_gy, n_gy, n_gx, n_gx, n_gy, n_gy)],
            compiler_params=params,
        )(*arguments)
    else:
        filtered, stacked = pl.pallas_call(
            functools.partial(filter_kernel, sizes),
            out_shape=[
                jax.ShapeDtypeStruct((2, ROWS, 128), F32),
                jax.ShapeDtypeStruct((384, 128), F32),
            ],
            in_specs=[hbm] * 5,
            out_specs=[vmem] * 2,
            scratch_shapes=filter_scratch,
            compiler_params=params,
        )(*arguments)
        stacked = lax.psum(stacked, ("gx", "gy"))
        result = pl.pallas_call(
            functools.partial(rotate_kernel, node_total),
            out_shape=jax.ShapeDtypeStruct(nodes.shape, BF16),
            in_specs=[vmem] * 2,
            out_specs=vmem,
            scratch_shapes=[pltpu.VMEM((2, 528, 128), F32), pltpu.VMEM((2, 528, 256), BF16)],
            compiler_params=pltpu.CompilerParams(vmem_limit_bytes=VMEM_BYTES),
        )(filtered, stacked)
    return jnp.transpose(result, (0, 2, 1, 3))


def solution(mesh):
    return jax.shard_map(
        body,
        mesh=mesh,
        in_specs=(P("gx", "gy", None, None), P("gx", "gy", None), P("gx", "gy", None, None, None)),
        out_specs=P("gx", "gy", None, None),
        check_vma=False,
    )
```
